512 devices in a mesh: angle: 128 (over y, x_hi, z), tile: 4 (over x_lo, core).
Axes of the slice: x: 4 (x_hi: 2, x_lo: 2; x = x_hi * 2 + x_lo), y: 4, z: 16, core: 2. Of those that a mesh axis runs over, the one named last changes fastest.
Arguments:
- projection: float32 [2, 128, 1024, 512], P(None, 'angle', 'tile'), may hold values from -5 to 5
- probe: float32 [2, 128, 128], replicated, may hold values from -5 to 5
- amplitude: float32 [128, 16, 128, 128], P('angle', 'tile'), may hold values from 0.4 to 2.2
- pos_row: int32 [128, 16], P('angle', 'tile'), may hold values from 0 to 255
- pos_col: int32 [128, 16], P('angle', 'tile'), may hold values from 0 to 384
- ang_offset: int32 [128], replicated, may hold values from 0 to 124, as said below
- ang_weight: float32 [128, 4], replicated, may hold values from 0.1 to 0.6
- det_offset: int32 [256], replicated, may hold values from 0 to 508, as said below
- det_weight: float32 [256, 4], replicated, may hold values from 0.1 to 0.6
Outputs:
- updated_projection: float32 [2, 128, 1024, 512], P(None, 'angle', 'tile')
- probe_direction: float32 [2, 128, 128], replicated
- volume: float32 [2, 4, 256, 128, 256], P(None, 'tile', 'angle')
The draws below stay inside these ranges and needn't reach their ends.
Inputs may be any that keep to these rules, and one draw needn't show every extreme that they name: `ang_offset`: regular angle r's band starts within one of r - 1, clipped to the valid range; both ends are reached. `det_offset`: radial sample q's band starts within one of 2 q - 1, clipped to the valid range; both ends are reached.
All inputs are finite; a program needn't handle non-finite values.
Results may differ from the reference program's by a relative error of at most 0.00011.
Values sent between devices are 32-bit elements; how exact they have to be, the bound alone decides.
No kernel may reach another device: no remote copies, remote signals or barrier semaphores. Data moves between devices by JAX's collectives and lax.ppermute only.
A program may use at most 64 MiB of HBM per device.

```python
import math
import jax
import jax.numpy as jnp
from jax import lax

P_SIZE = 128
W = 512
TILE_ROWS = 256
PAT_DEV = 4
HALF = 64
ANGLES = 128
PATCHES = 16
H = 1024
NREG = 128
NR = 256
N_TILE = 4


def draw_ang_offset(key, part):
    jitter = jax.random.randint(key, (NREG,), -1, 2)
    base_rows = jnp.arange(NREG, dtype=jnp.int32) - 1 + jitter
    return jnp.clip(base_rows, 0, ANGLES - 4).astype(jnp.int32)


def draw_det_offset(key, part):
    jitter = jax.random.randint(jax.random.fold_in(key, 7), (NR,), -1, 2)
    base_rows = 2 * jnp.arange(NR, dtype=jnp.int32) - 1 + jitter
    return jnp.clip(base_rows, 0, W - 4).astype(jnp.int32)


def with_ends(array, own_key, smallest, high):
    longest = array.shape.index(max(array.shape))
    spots = []
    for shift in (0, 1):
        where = [jax.random.randint(jax.random.fold_in(own_key, axis), (), 0, length) for axis, length in enumerate(array.shape)]
        where[longest] = (where[longest] + shift) % array.shape[longest]
        spots.append(tuple(where))
    return array.at[spots[0]].set(smallest).at[spots[1]].set(high)


def level_of(rng, shape, cuts, smallest, top_value):
    def one(dim, parts):
        heights = jax.random.uniform(jax.random.fold_in(jax.random.fold_in(rng, 6), dim), (parts,), jnp.float32, smallest / len(cuts), top_value / len(cuts))
        return jnp.repeat(jnp.exp(heights), shape[dim] // parts).reshape((-1,) + (1,) * (len(shape) - dim - 1))

    level = one(*cuts[0])
    for cut in cuts[1:]:
        level = level * one(*cut)
    return level


def normal_values(stream_key, extent, width, limit, cuts=(), held_as=jnp.bfloat16):
    result = jax.random.normal(stream_key, extent, jnp.float32) * width
    if len(cuts) > 0:
        result = level_of(stream_key, extent, cuts, -0.22, 0.18) * result
    return jnp.clip(result, min=-limit, max=limit).astype(held_as)


def setup_inputs(seed: int = 0) -> dict:
    seeds = jax.random.split(jax.random.key(seed), 10)
    projection = normal_values(seeds[0], (2, ANGLES, H, W), 0.7, 5.0, ((1, 128), (2, 4)), jnp.float32)
    probe = normal_values(seeds[1], (2, P_SIZE, P_SIZE), 0.7, 5.0, (), jnp.float32)
    amplitude = jnp.clip(0.4 + 1.80000004 * jax.random.uniform(seeds[2], (ANGLES, PATCHES, P_SIZE, P_SIZE), jnp.float32) ** level_of(seeds[2], (ANGLES, PATCHES, P_SIZE, P_SIZE), ((0, 128), (1, 4)), -0.2, 0.2), 0.4, 2.2)
    pos_row = with_ends(jax.random.randint(seeds[3], (ANGLES, PATCHES), 0, TILE_ROWS), jax.random.fold_in(seeds[3], 1), 0, TILE_ROWS - 1).astype(jnp.int32)
    pos_col = with_ends(jax.random.randint(seeds[4], (ANGLES, PATCHES), 0, W - P_SIZE + 1), jax.random.fold_in(seeds[4], 1), 0, W - P_SIZE).astype(jnp.int32)
    ang_offset = draw_ang_offset(jax.random.fold_in(seeds[9], 71), 0)
    ang_weight = jnp.clip(jax.random.uniform(seeds[6], (NREG, 4), jnp.float32, 0.1, 0.6), 0.1, 0.6)
    det_offset = draw_det_offset(jax.random.fold_in(seeds[9], 71), 0)
    det_weight = jnp.clip(jax.random.uniform(seeds[8], (NR, 4), jnp.float32, 0.1, 0.6), 0.1, 0.6)
    return {"projection": projection, "probe": probe, "amplitude": amplitude, "pos_row": pos_row, "pos_col": pos_col, "ang_offset": ang_offset, "ang_weight": ang_weight, "det_offset": det_offset, "det_weight": det_weight}


STEP_SIZE = 0.1
EPSILON = 1e-06
HIGHEST = lax.Precision.HIGHEST

def dft_tables(length):
    counter = jnp.arange(length, dtype=jnp.int32)
    product_mod = counter[:, None] * counter[None, :] % length
    angle_table = product_mod.astype(jnp.float32) * (2.0 * math.pi / length)
    norm_scale = 1.0 / math.sqrt(length)
    return (jnp.cos(angle_table) * norm_scale, -jnp.sin(angle_table) * norm_scale)

def transform(values_re, values_im, table_re, table_im):
    left_re = jnp.einsum('ij,bjk->bik', table_re, values_re, precision=HIGHEST) - jnp.einsum('ij,bjk->bik', table_im, values_im, precision=HIGHEST)
    left_im = jnp.einsum('ij,bjk->bik', table_re, values_im, precision=HIGHEST) + jnp.einsum('ij,bjk->bik', table_im, values_re, precision=HIGHEST)
    right_re = jnp.einsum('bij,jk->bik', left_re, table_re, precision=HIGHEST) - jnp.einsum('bij,jk->bik', left_im, table_im, precision=HIGHEST)
    right_im = jnp.einsum('bij,jk->bik', left_re, table_im, precision=HIGHEST) + jnp.einsum('bij,jk->bik', left_im, table_re, precision=HIGHEST)
    return (right_re, right_im)

def patch_terms(object_re, object_im, amp_block, probe_re, probe_im, cosine_table, sine_table):
    exit_re = probe_re * object_re - probe_im * object_im
    exit_im = probe_re * object_im + probe_im * object_re
    spec_re, spec_im = transform(exit_re, exit_im, cosine_table, sine_table)
    magnitude = jnp.sqrt(spec_re * spec_re + spec_im * spec_im)
    factor = 1.0 - amp_block / jnp.maximum(magnitude, 1.0)
    back_re, back_im = transform(spec_re * factor, spec_im * factor, cosine_table, -sine_table)
    grad_re = probe_re * back_re + probe_im * back_im
    grad_im = probe_re * back_im - probe_im * back_re
    term_re = lax.optimization_barrier(jnp.sum(object_re * back_re + object_im * back_im, axis=0))
    term_im = lax.optimization_barrier(jnp.sum(object_re * back_im - object_im * back_re, axis=0))
    weight_sum = lax.optimization_barrier(jnp.sum(object_re * object_re + object_im * object_im, axis=0))
    return (grad_re, grad_im, term_re, term_im, weight_sum)

def band_matrix(offset, weight, length):
    columns = jnp.arange(length, dtype=jnp.int32)
    matrix = jnp.zeros((offset.shape[0], length), jnp.float32)
    for band_step in range(weight.shape[1]):
        hits = (columns[None, :] == offset[:, None] + band_step).astype(jnp.float32)
        matrix = matrix + weight[:, band_step:band_step + 1] * hits
    return matrix

def reference(projection, probe, amplitude, pos_row, pos_col, ang_offset, ang_weight, det_offset, det_weight):
    cosine_table, sine_table = dft_tables(P_SIZE)
    probe_re = probe[0]
    probe_im = probe[1]
    padded = jnp.pad(projection, ((0, 0), (0, 0), (HALF, HALF), (0, 0)))
    padded = jnp.moveaxis(padded, 1, 0)
    owners = jnp.arange(PATCHES, dtype=jnp.int32) // PAT_DEV

    def one_angle(carried, inputs):
        plane_data, row_here, col_here, amp_here = inputs
        starts = owners * TILE_ROWS + row_here

        def cut_patch(start_row, start_col):
            return lax.dynamic_slice(plane_data, (jnp.int32(0), start_row, start_col), (2, P_SIZE, P_SIZE))
        pieces = jax.vmap(cut_patch)(starts, col_here)
        grad_re, grad_im, term_re, term_im, weight_sum = patch_terms(pieces[:, 0], pieces[:, 1], amp_here, probe_re, probe_im, cosine_table, sine_table)

        def deposit(number, accumulated):
            corner = (jnp.int32(0), starts[number], col_here[number])
            window = lax.dynamic_slice(accumulated, corner, (2, P_SIZE, P_SIZE))
            addend = jnp.stack([grad_re[number], grad_im[number]])
            return lax.dynamic_update_slice(accumulated, window + addend, corner)
        gradient = lax.fori_loop(0, PATCHES, deposit, jnp.zeros_like(plane_data))
        summed = (carried[0] + term_re, carried[1] + term_im, carried[2] + weight_sum)
        return (summed, gradient)
    zeros_pp = jnp.zeros((P_SIZE, P_SIZE), jnp.float32)
    sums, stacked = lax.scan(one_angle, (zeros_pp, zeros_pp, zeros_pp), (padded, pos_row, pos_col, amplitude))
    gradient = jnp.moveaxis(stacked, 0, 1)[:, :, HALF:HALF + H]
    updated = projection - STEP_SIZE * gradient
    norm_scale = lax.rsqrt(sums[2] + EPSILON)
    direction = jnp.stack([sums[0] * norm_scale, sums[1] * norm_scale])
    det_matrix = band_matrix(det_offset, det_weight, W)
    ang_matrix = band_matrix(ang_offset, ang_weight, ANGLES)
    resampled = jnp.einsum('cahw,qw->cahq', updated, det_matrix, precision=HIGHEST)
    volume = jnp.einsum('ra,cahq->chrq', ang_matrix, resampled, precision=HIGHEST)
    volume = volume.reshape(2, N_TILE, TILE_ROWS, NREG, NR)
    return (updated, direction, volume)
```

```python
import functools

import jax
import jax.numpy as jnp
import numpy as np
from jax import lax
from jax.experimental import pallas as pl
from jax.experimental.pallas import tpu as pltpu
from jax.sharding import PartitionSpec as P

STEP_SIZE = 0.1
EPSILON = 1e-06
F32 = jnp.float32
BF16 = jnp.bfloat16


def complex_table(length):
    counter = np.arange(length)
    angle = (counter[:, None] * counter[None, :] % length) * (2.0 * np.pi / length)
    re = np.cos(angle) / np.sqrt(length)
    im = -np.sin(angle) / np.sqrt(length)
    table = np.block([[re, -im], [im, re]]).astype(np.float32)
    high = table.astype(BF16)
    low = (table - high.astype(np.float32)).astype(BF16)
    return high, low


def split(value):
    high = value.astype(BF16)
    low = (value - high.astype(F32)).astype(BF16)
    return high, low


def dot3(left, right):
    mul = functools.partial(jnp.dot, preferred_element_type=F32)
    return mul(left[0], right[0]) + (mul(left[0], right[1]) + mul(left[1], right[0]))


def patch_kernel(
    row_ref, col_ref, cur_ref, before_ref, after_ref, probe_ref, amp_ref,
    gh_ref, gl_ref, th_ref, tl_ref,
    own_ref, up_ref, down_ref, term_ref,
    padded, grad, objects, tall, wide,
):
    side = probe_ref.shape[-1]
    half = side // 2
    rows = cur_ref.shape[1]
    lanes = cur_ref.shape[2]
    count = amp_ref.shape[0]
    window = 2 * side
    tall_side = side + 8

    padded[:, :half] = before_ref[...]
    padded[:, half : half + rows] = cur_ref[...]
    padded[:, half + rows :] = after_ref[...]
    grad[...] = jnp.zeros(grad.shape, F32)

    def place(k):
        row = row_ref[0, k]
        col = col_ref[0, k]
        first = lax.div(row, 8)
        base = jnp.minimum(lax.div(col, side), lanes // side - 2)
        where = (
            pl.ds(pl.multiple_of(first * 8, 8), tall_side),
            pl.ds(pl.multiple_of(base * side, side), window),
        )
        return where, row - first * 8, col - base * side

    probe_re = probe_ref[0]
    probe_im = probe_ref[1]
    for k in range(count):
        where, row_shift, col_shift = place(k)
        row_back = lax.rem(tall_side - row_shift, tall_side)
        col_back = lax.rem(window - col_shift, window)
        for c in range(2):
            block = padded[(c,) + where]
            block = pltpu.roll(block, col_back, 1)[:, :side]
            objects[k, c] = pltpu.roll(block, row_back, 0)[:side]
        o_re = objects[k, 0]
        o_im = objects[k, 1]
        here = slice(k * side, (k + 1) * side)
        tall[:side, here] = probe_re * o_re - probe_im * o_im
        tall[side:, here] = probe_re * o_im + probe_im * o_re

    table = (gh_ref[...], gl_ref[...])
    flipped = (th_ref[...], tl_ref[...])

    left = dot3(table, split(tall[...]))
    for k in range(count):
        here = slice(k * side, (k + 1) * side)
        wide[here, :side] = left[:side, here]
        wide[here, side:] = left[side:, here]
    spec = dot3(split(wide[...]), flipped)
    for k in range(count):
        here = slice(k * side, (k + 1) * side)
        s_re = spec[here, :side]
        s_im = spec[here, side:]
        norm = lax.rsqrt(jnp.maximum(s_re * s_re + s_im * s_im, 1.0))
        factor = 1.0 - amp_ref[k] * norm
        tall[:side, here] = s_re * factor
        tall[side:, here] = s_im * factor
    left = dot3(flipped, split(tall[...]))
    for k in range(count):
        here = slice(k * side, (k + 1) * side)
        wide[here, :side] = left[:side, here]
        wide[here, side:] = left[side:, here]
    wide[...] = dot3(split(wide[...]), table)

    term_re = jnp.zeros((side, side), F32)
    term_im = jnp.zeros((side, side), F32)
    weight = jnp.zeros((side, side), F32)
    for k in range(count):
        here = slice(k * side, (k + 1) * side)
        o_re = objects[k, 0]
        o_im = objects[k, 1]
        b_re = wide[here, :side]
        b_im = wide[here, side:]
        term_re = term_re + (o_re * b_re + o_im * b_im)
        term_im = term_im + (o_re * b_im - o_im * b_re)
        weight = weight + (o_re * o_re + o_im * o_im)
        where, row_shift, col_shift = place(k)
        pair = (probe_re * b_re + probe_im * b_im, probe_re * b_im - probe_im * b_re)
        for c in range(2):
            block = jnp.concatenate([pair[c], jnp.zeros((8, side), F32)], axis=0)
            block = pltpu.roll(block, row_shift, 0)
            block = jnp.concatenate([block, jnp.zeros((tall_side, side), F32)], axis=1)
            block = pltpu.roll(block, col_shift, 1)
            grad[(c,) + where] = grad[(c,) + where] + block
    term_ref[:, :side] = term_re
    term_ref[:, side : 2 * side] = term_im
    term_ref[:, 2 * side :] = weight
    up_ref[...] = grad[:, :half]
    down_ref[...] = grad[:, half + rows :]
    own_ref[...] = cur_ref[...] - STEP_SIZE * grad[:, half : half + rows]


def update_kernel(own_ref, above_ref, below_ref, dh_ref, dl_ref, updated_ref, send_ref, whole, sheet):
    half = above_ref.shape[1]
    rows = own_ref.shape[1]
    per = send_ref.shape[1] // 4
    whole[:, half : rows - half] = own_ref[:, half : rows - half]
    whole[:, :half] = own_ref[:, :half] - STEP_SIZE * above_ref[...]
    whole[:, rows - half :] = own_ref[:, rows - half :] - STEP_SIZE * below_ref[...]
    updated_ref[...] = whole[...]
    table = (dh_ref[...], dl_ref[...])
    for c in range(2):
        product = dot3(split(whole[c]), table)
        for part in range(per // 128):
            sheet[part] = product[:, part * 128 : (part + 1) * 128]
        for s in range(2):
            for part in range(per // 128):
                where = (2 * c + s) * per + part * 128
                send_ref[:, where : where + 128] = sheet[part, pl.ds(s, rows // 2, stride=2), :]


def volume_kernel(arrived_ref, ah_ref, al_ref, volume_ref, direction_ref):
    per = volume_ref.shape[-1]
    side = direction_ref.shape[-1]
    for c in range(2):
        where = 4 * per + c * side
        direction_ref[c] = arrived_ref[:, where : where + side]
    table = (ah_ref[...], al_ref[...])
    for c in range(2):
        for s in range(2):
            where = (2 * c + s) * per
            block = arrived_ref[:, where : where + per]
            volume_ref[c, s] = dot3(table, split(block))


def band(offset, weight, length):
    column = lax.broadcasted_iota(jnp.int32, (length, offset.shape[1]), 0)
    matrix = jnp.zeros(column.shape, F32)
    for step in range(weight.shape[0]):
        matrix = jnp.where(column == offset + step, weight[step : step + 1], matrix)
    return matrix


def band_kernel(do_ref, dw_ref, ao_ref, aw_ref, dh_ref, dl_ref, ah_ref, al_ref):
    dh_ref[...], dl_ref[...] = split(band(do_ref[...], dw_ref[...], dh_ref.shape[0]))
    turned = band(ao_ref[...], aw_ref[...], ah_ref.shape[1])
    ah_ref[...], al_ref[...] = split(turned.T)


def vmem(count):
    return [pl.BlockSpec(memory_space=pltpu.VMEM)] * count


def local(
    projection, probe, amplitude, pos_row, pos_col, ang_offset, ang_weight, det_offset, det_weight
):
    side = probe.shape[-1]
    half = side // 2
    rows = projection.shape[2]
    lanes = projection.shape[3]
    count = amplitude.shape[1]
    angles = lax.axis_size("angle")
    tiles = lax.axis_size("tile")
    radial = det_offset.shape[0]
    up = [(i, i + 1) for i in range(tiles - 1)]
    down = [(i + 1, i) for i in range(tiles - 1)]

    current = projection[:, 0]
    shape = jax.ShapeDtypeStruct
    before = lax.ppermute(current[:, rows - half :], "tile", up)
    after = lax.ppermute(current[:, :half], "tile", down)

    regular = ang_offset.shape[0]
    det_high, det_low, ang_high, ang_low = pl.pallas_call(
        band_kernel,
        out_shape=(shape((lanes, radial), BF16),) * 2 + (shape((regular, angles), BF16),) * 2,
        in_specs=vmem(4),
        out_specs=tuple(vmem(4)),
        name="bands",
    )(det_offset[None], det_weight.T, ang_offset[None], ang_weight.T)

    high, low = complex_table(side)
    own, upper, lower, terms = pl.pallas_call(
        patch_kernel,
        out_shape=(
            shape((2, rows, lanes), F32),
            shape((2, half, lanes), F32),
            shape((2, half, lanes), F32),
            shape((side, 3 * side), F32),
        ),
        in_specs=[pl.BlockSpec(memory_space=pltpu.SMEM)] * 2 + vmem(9),
        out_specs=tuple(vmem(4)),
        scratch_shapes=[
            pltpu.VMEM((2, rows + 2 * half, lanes), F32),
            pltpu.VMEM((2, rows + 2 * half, lanes), F32),
            pltpu.VMEM((count, 2, side, side), F32),
            pltpu.VMEM((2 * side, count * side), F32),
            pltpu.VMEM((count * side, 2 * side), F32),
        ],
        name="patches",
    )(
        pos_row, pos_col, current, before, after, probe, amplitude[0],
        jnp.asarray(high), jnp.asarray(low), jnp.asarray(high.T), jnp.asarray(low.T),
    )

    below = lax.ppermute(upper, "tile", down)
    above = lax.ppermute(lower, "tile", up)

    shares = lax.all_to_all(terms, "angle", 0, 0, tiled=True)

    updated, outgoing = pl.pallas_call(
        update_kernel,
        out_shape=(shape((2, rows, lanes), F32), shape((rows // 2, 4 * radial), F32)),
        in_specs=vmem(5),
        out_specs=tuple(vmem(2)),
        scratch_shapes=[
            pltpu.VMEM((2, rows, lanes), F32),
            pltpu.VMEM((radial // 128, rows, 128), F32),
        ],
        name="update",
    )(own, above, below, det_high, det_low)

    total = jnp.sum(shares, axis=0, keepdims=True)
    step = 1
    while step < tiles:
        pairs = [(i, i ^ step) for i in range(tiles)]
        total = total + lax.ppermute(total, "tile", pairs)
        step *= 2
    scale = lax.rsqrt(total[:, 2 * side :] + EPSILON)
    line = jnp.concatenate(
        [total[:, :side] * scale, total[:, side : 2 * side] * scale], axis=1
    )

    line = jnp.broadcast_to(line, (angles, 2 * side))
    arrived = lax.all_to_all(jnp.concatenate([outgoing, line], axis=1), "angle", 0, 0, tiled=True)

    volume, direction = pl.pallas_call(
        volume_kernel,
        out_shape=(shape((2, 2, regular, radial), F32), shape((2, side, side), F32)),
        in_specs=vmem(3),
        out_specs=tuple(vmem(2)),
        name="volume",
    )(arrived, ang_high, ang_low)
    return (updated[:, None], direction, volume[:, None])


def solution(mesh):
    in_specs = (
        P(None, "angle", "tile", None),
        P(),
        P("angle", "tile", None, None),
        P("angle", "tile"),
        P("angle", "tile"),
        P(),
        P(),
        P(),
        P(),
    )
    out_specs = (P(None, "angle", "tile", None), P(), P(None, "tile", "angle", None, None))
    return jax.shard_map(local, mesh=mesh, in_specs=in_specs, out_specs=out_specs, check_vma=False)
```

```python
import functools

import jax
import jax.numpy as jnp
import numpy as np
from jax import lax
from jax.experimental import pallas as pl
from jax.experimental.pallas import tpu as pltpu
from jax.sharding import PartitionSpec as P

STEP_SIZE = 0.1
EPSILON = 1e-06
F32 = jnp.float32
BF16 = jnp.bfloat16


def complex_table(length):
    counter = np.arange(length)
    angle = (counter[:, None] * counter[None, :] % length) * (2.0 * np.pi / length)
    re = np.cos(angle) / np.sqrt(length)
    im = -np.sin(angle) / np.sqrt(length)
    table = np.block([[re, -im], [im, re]]).astype(np.float32)
    high = table.astype(BF16)
    low = (table - high.astype(np.float32)).astype(BF16)
    return high, low


def split(value):
    high = value.astype(BF16)
    low = (value - high.astype(F32)).astype(BF16)
    return high, low


def dot3(left, right):
    mul = functools.partial(jnp.dot, preferred_element_type=F32)
    return mul(left[0], right[0]) + (mul(left[0], right[1]) + mul(left[1], right[0]))


def patch_kernel(
    row_ref, col_ref, cur_ref, before_ref, after_ref, probe_ref, amp_ref,
    gh_ref, gl_ref, th_ref, tl_ref,
    own_ref, up_ref, down_ref, term_ref,
    padded, grad, objects, tall, wide,
):
    side = probe_ref.shape[-1]
    half = side // 2
    rows = cur_ref.shape[1]
    lanes = cur_ref.shape[2]
    count = amp_ref.shape[0]
    window = 2 * side
    tall_side = side + 8

    padded[:, :half] = before_ref[...]
    padded[:, half : half + rows] = cur_ref[...]
    padded[:, half + rows :] = after_ref[...]
    grad[...] = jnp.zeros(grad.shape, F32)

    def place(k):
        row = row_ref[0, k]
        col = col_ref[0, k]
        first = lax.div(row, 8)
        base = jnp.minimum(lax.div(col, side), lanes // side - 2)
        where = (
            pl.ds(pl.multiple_of(first * 8, 8), tall_side),
            pl.ds(pl.multiple_of(base * side, side), window),
        )
        return where, row - first * 8, col - base * side

    probe_re = probe_ref[0]
    probe_im = probe_ref[1]
    for k in range(count):
        where, row_shift, col_shift = place(k)
        row_back = lax.rem(tall_side - row_shift, tall_side)
        col_back = lax.rem(window - col_shift, window)
        for c in range(2):
            block = padded[(c,) + where]
            block = pltpu.roll(block, col_back, 1)[:, :side]
            objects[k, c] = pltpu.roll(block, row_back, 0)[:side]
        o_re = objects[k, 0]
        o_im = objects[k, 1]
        here = slice(k * side, (k + 1) * side)
        tall[:side, here] = probe_re * o_re - probe_im * o_im
        tall[side:, here] = probe_re * o_im + probe_im * o_re

    table = (gh_ref[...], gl_ref[...])
    flipped = (th_ref[...], tl_ref[...])

    left = dot3(table, split(tall[...]))
    for k in range(count):
        here = slice(k * side, (k + 1) * side)
        wide[here, :side] = left[:side, here]
        wide[here, side:] = left[side:, here]
    spec = dot3(split(wide[...]), flipped)
    for k in range(count):
        here = slice(k * side, (k + 1) * side)
        s_re = spec[here, :side]
        s_im = spec[here, side:]
        norm = lax.rsqrt(jnp.maximum(s_re * s_re + s_im * s_im, 1.0))
        factor = 1.0 - amp_ref[k] * norm
        tall[:side, here] = s_re * factor
        tall[side:, here] = s_im * factor
    left = dot3(flipped, split(tall[...]))
    for k in range(count):
        here = slice(k * side, (k + 1) * side)
        wide[here, :side] = left[:side, here]
        wide[here, side:] = left[side:, here]
    wide[...] = dot3(split(wide[...]), table)

    term_re = jnp.zeros((side, side), F32)
    term_im = jnp.zeros((side, side), F32)
    weight = jnp.zeros((side, side), F32)
    for k in range(count):
        here = slice(k * side, (k + 1) * side)
        o_re = objects[k, 0]
        o_im = objects[k, 1]
        b_re = wide[here, :side]
        b_im = wide[here, side:]
        term_re = term_re + (o_re * b_re + o_im * b_im)
        term_im = term_im + (o_re * b_im - o_im * b_re)
        weight = weight + (o_re * o_re + o_im * o_im)
        where, row_shift, col_shift = place(k)
        pair = (probe_re * b_re + probe_im * b_im, probe_re * b_im - probe_im * b_re)
        for c in range(2):
            block = jnp.concatenate([pair[c], jnp.zeros((8, side), F32)], axis=0)
            block = pltpu.roll(block, row_shift, 0)
            block = jnp.concatenate([block, jnp.zeros((tall_side, side), F32)], axis=1)
            block = pltpu.roll(block, col_shift, 1)
            grad[(c,) + where] = grad[(c,) + where] + block
    tiles = term_ref.shape[0] // side
    part = side // tiles
    lane = lax.broadcasted_iota(jnp.int32, (side, side), 1)
    for t in range(tiles):
        share = pltpu.roll(weight, (2 * part - part * t) % side, 1)
        share = jnp.where(lane < 2 * part, pltpu.roll(term_im, (part - part * t) % side, 1), share)
        share = jnp.where(lane < part, pltpu.roll(term_re, -part * t % side, 1), share)
        term_ref[pl.ds(t, side, stride=tiles), :] = share
    up_ref[...] = grad[:, :half]
    down_ref[...] = grad[:, half + rows :]
    own_ref[...] = cur_ref[...] - STEP_SIZE * grad[:, half : half + rows]


def update_kernel(own_ref, above_ref, below_ref, dh_ref, dl_ref, updated_ref, send_ref, whole, sheet):
    half = above_ref.shape[1]
    rows = own_ref.shape[1]
    per = dh_ref.shape[1]
    pieces = send_ref.shape[0] // (rows // 2)
    whole[:, half : rows - half] = own_ref[:, half : rows - half]
    whole[:, :half] = own_ref[:, :half] - STEP_SIZE * above_ref[...]
    whole[:, rows - half :] = own_ref[:, rows - half :] - STEP_SIZE * below_ref[...]
    updated_ref[...] = whole[...]
    table = (dh_ref[...], dl_ref[...])
    for c in range(2):
        product = dot3(split(whole[c]), table)
        for part in range(per // 128):
            sheet[part] = product[:, part * 128 : (part + 1) * 128]
        for s in range(2):
            for part in range(per // 128):
                piece = (2 * c + s) * (per // 128) + part
                rows_of = pl.ds(piece, rows // 2, stride=pieces)
                send_ref[rows_of, :] = sheet[part, pl.ds(s, rows // 2, stride=2), :]


def line_kernel(share_ref, packed_ref, sent_ref):
    lanes = share_ref.shape[1]
    part = lanes // 4
    total = jnp.sum(share_ref[...], axis=0, keepdims=True)
    total = jnp.broadcast_to(total, (8, lanes))
    lane = lax.broadcasted_iota(jnp.int32, (8, lanes), 1)
    weight = jnp.where(
        lane < part, pltpu.roll(total, lanes - 2 * part, 1), pltpu.roll(total, lanes - part, 1)
    )
    line = jnp.where(lane < 2 * part, total * lax.rsqrt(weight + EPSILON), 0.0)
    peers = lanes
    pieces = sent_ref.shape[0] // peers
    sent_ref[...] = packed_ref[...]
    sent_ref[pl.ds(pieces - 1, peers, stride=pieces), :] = jnp.broadcast_to(line[:1], (peers, lanes))


def volume_kernel(arrived_ref, ah_ref, al_ref, volume_ref):
    parts = volume_ref.shape[-1] // 128
    angles = ah_ref.shape[1]
    pieces = arrived_ref.shape[0] // angles
    table = (ah_ref[...], al_ref[...])
    for c in range(2):
        for s in range(2):
            blocks = [
                arrived_ref[pl.ds((2 * c + s) * parts + part, angles, stride=pieces), :]
                for part in range(parts)
            ]
            volume_ref[c, s] = dot3(table, split(jnp.concatenate(blocks, axis=1)))


def direction_kernel(me_ref, *refs):
    direction_ref = refs[-1]
    side = direction_ref.shape[-1]
    tiles = len(refs) - 1
    part = side // tiles
    lane = lax.broadcasted_iota(jnp.int32, (side, side), 1)
    whole = [jnp.zeros((side, side), F32)] * 2
    for k in range(tiles):
        source = lax.rem(me_ref[0] + tiles - k, tiles)
        here = (lane >= source * part) & (lane < (source + 1) * part)
        for c in range(2):
            shift = lax.rem(source * part + side - c * part, side)
            whole[c] = jnp.where(here, pltpu.roll(refs[k][...], shift, 1), whole[c])
    for c in range(2):
        direction_ref[c] = whole[c]


def band(offset, weight, length):
    column = lax.broadcasted_iota(jnp.int32, (length, offset.shape[1]), 0)
    matrix = jnp.zeros(column.shape, F32)
    for step in range(weight.shape[0]):
        matrix = jnp.where(column == offset + step, weight[step : step + 1], matrix)
    return matrix


def band_kernel(do_ref, dw_ref, ao_ref, aw_ref, dh_ref, dl_ref, ah_ref, al_ref):
    dh_ref[...], dl_ref[...] = split(band(do_ref[...], dw_ref[...], dh_ref.shape[0]))
    turned = band(ao_ref[...], aw_ref[...], ah_ref.shape[1])
    ah_ref[...], al_ref[...] = split(turned.T)


def held(value):
    return pltpu.with_memory_space_constraint(value, pltpu.VMEM)


def vmem(count):
    return [pl.BlockSpec(memory_space=pltpu.VMEM)] * count


def local(
    projection, probe, amplitude, pos_row, pos_col, ang_offset, ang_weight, det_offset, det_weight
):
    side = probe.shape[-1]
    half = side // 2
    rows = projection.shape[2]
    lanes = projection.shape[3]
    count = amplitude.shape[1]
    angles = lax.axis_size("angle")
    tiles = lax.axis_size("tile")
    radial = det_offset.shape[0]
    up = [(i, i + 1) for i in range(tiles - 1)]
    down = [(i + 1, i) for i in range(tiles - 1)]

    current = projection[:, 0]
    shape = jax.ShapeDtypeStruct
    before = lax.ppermute(current[:, rows - half :], "tile", up)
    after = lax.ppermute(current[:, :half], "tile", down)

    regular = ang_offset.shape[0]
    det_high, det_low, ang_high, ang_low = pl.pallas_call(
        band_kernel,
        out_shape=(pltpu.VMEM((lanes, radial), BF16),) * 2
        + (pltpu.VMEM((regular, angles), BF16),) * 2,
        in_specs=vmem(4),
        out_specs=tuple(vmem(4)),
        name="bands",
    )(det_offset[None], det_weight.T, ang_offset[None], ang_weight.T)

    high, low = complex_table(side)
    own, upper, lower, terms = pl.pallas_call(
        patch_kernel,
        out_shape=(
            shape((2, rows, lanes), F32),
            pltpu.VMEM((2, half, lanes), F32),
            pltpu.VMEM((2, half, lanes), F32),
            pltpu.VMEM((side * tiles, side), F32),
        ),
        in_specs=[pl.BlockSpec(memory_space=pltpu.SMEM)] * 2 + vmem(9),
        out_specs=tuple(vmem(4)),
        scratch_shapes=[
            pltpu.VMEM((2, rows + 2 * half, lanes), F32),
            pltpu.VMEM((2, rows + 2 * half, lanes), F32),
            pltpu.VMEM((count, 2, side, side), F32),
            pltpu.VMEM((2 * side, count * side), F32),
            pltpu.VMEM((count * side, 2 * side), F32),
        ],
        name="patches",
    )(
        pos_row, pos_col, current, held(before), held(after), probe, amplitude[0],
        jnp.asarray(high), jnp.asarray(low), jnp.asarray(high.T), jnp.asarray(low.T),
    )

    shares = lax.all_to_all(terms, ("angle", "tile"), 0, 0, tiled=True)

    below = lax.ppermute(upper, "tile", down)
    above = lax.ppermute(lower, "tile", up)

    peers = rows // 2
    pieces = 4 * radial // 128 + 1
    updated, packed = pl.pallas_call(
        update_kernel,
        out_shape=(shape((2, rows, lanes), F32), pltpu.VMEM((peers * pieces, 128), F32)),
        in_specs=vmem(5),
        out_specs=tuple(vmem(2)),
        scratch_shapes=[
            pltpu.VMEM((2, rows, lanes), F32),
            pltpu.VMEM((radial // 128, rows, 128), F32),
        ],
        name="update",
    )(own, held(above), held(below), held(det_high), held(det_low))

    sent = pl.pallas_call(
        line_kernel,
        out_shape=pltpu.VMEM((peers * pieces, 128), F32),
        in_specs=vmem(2),
        out_specs=vmem(1)[0],
        name="line",
    )(held(shares), held(packed))

    arrived = lax.all_to_all(
        sent.reshape(peers, pieces * 128), "angle", 0, 0, tiled=True
    )

    mine = lax.slice(
        arrived.reshape(peers * pieces, 128),
        (pieces - 1, 0), (peers * pieces, 128), (pieces, 1),
    )
    quarters = [mine] + [
        lax.ppermute(mine, "tile", [(i, (i + k) % tiles) for i in range(tiles)])
        for k in range(1, tiles)
    ]
    volume = pl.pallas_call(
        volume_kernel,
        out_shape=shape((2, 2, regular, radial), F32),
        in_specs=vmem(3),
        out_specs=vmem(1)[0],
        name="volume",
    )(held(arrived.reshape(peers * pieces, 128)), held(ang_high), held(ang_low))
    direction = pl.pallas_call(
        direction_kernel,
        out_shape=shape((2, side, side), F32),
        in_specs=[pl.BlockSpec(memory_space=pltpu.SMEM)] + vmem(tiles),
        out_specs=vmem(1)[0],
        name="direction",
    )(lax.axis_index("tile")[None], *map(held, quarters))
    return (updated[:, None], direction, volume[:, None])


def solution(mesh):
    in_specs = (
        P(None, "angle", "tile", None),
        P(),
        P("angle", "tile", None, None),
        P("angle", "tile"),
        P("angle", "tile"),
        P(),
        P(),
        P(),
        P(),
    )
    out_specs = (P(None, "angle", "tile", None), P(), P(None, "tile", "angle", None, None))
    return jax.shard_map(local, mesh=mesh, in_specs=in_specs, out_specs=out_specs, check_vma=False)
```

```python
import functools

import jax
import jax.numpy as jnp
import numpy as np
from jax import lax
from jax.experimental import pallas as pl
from jax.experimental.pallas import tpu as pltpu
from jax.sharding import PartitionSpec as P

STEP_SIZE = 0.1
EPSILON = 1e-06
F32 = jnp.float32
BF16 = jnp.bfloat16


def complex_table(length):
    counter = np.arange(length)
    angle = (counter[:, None] * counter[None, :] % length) * (2.0 * np.pi / length)
    re = np.cos(angle) / np.sqrt(length)
    im = -np.sin(angle) / np.sqrt(length)
    table = np.block([[re, -im], [im, re]]).astype(np.float32)
    high = table.astype(BF16)
    low = (table - high.astype(np.float32)).astype(BF16)
    return high, low


def split(value):
    high = value.astype(BF16)
    low = (value - high.astype(F32)).astype(BF16)
    return high, low


def dot3(left, right):
    mul = functools.partial(jnp.dot, preferred_element_type=F32)
    return mul(left[0], right[0]) + (mul(left[0], right[1]) + mul(left[1], right[0]))


def places(row_ref, col_ref, k, side, lanes):
    row = row_ref[0, k]
    col = col_ref[0, k]
    first = lax.div(row, 8)
    base = jnp.minimum(lax.div(col, side), lanes // side - 2)
    where = (
        pl.ds(pl.multiple_of(first * 8, 8), side + 8),
        pl.ds(pl.multiple_of(base * side, side), 2 * side),
    )
    return where, row - first * 8, col - base * side


def terms_kernel(
    row_ref, col_ref, cur_ref, before_ref, after_ref, probe_in, amp_in, high_in, low_in,
    term_ref, back_ref,
    padded, objects, tall, wide, probe_ref, amp_ref, high_ref, low_ref, sems,
):
    side = probe_ref.shape[-1]
    half = side // 2
    rows = cur_ref.shape[1]
    lanes = cur_ref.shape[2]
    count = amp_ref.shape[0]
    loads = [
        pltpu.make_async_copy(source, target, sems.at[i])
        for i, (source, target) in enumerate(
            ((probe_in, probe_ref), (high_in, high_ref), (low_in, low_ref), (amp_in, amp_ref))
        )
    ]
    for load in loads:
        load.start()

    padded[:, :half] = before_ref[...]
    padded[:, half : half + rows] = cur_ref[...]
    padded[:, half + rows :] = after_ref[...]

    loads[0].wait()
    probe_re = probe_ref[0]
    probe_im = probe_ref[1]
    for k in range(count):
        where, row_shift, col_shift = places(row_ref, col_ref, k, side, lanes)
        row_back = lax.rem(side + 8 - row_shift, side + 8)
        col_back = lax.rem(2 * side - col_shift, 2 * side)
        for c in range(2):
            block = padded[(c,) + where]
            block = pltpu.roll(block, col_back, 1)[:, :side]
            objects[k, c] = pltpu.roll(block, row_back, 0)[:side]
        o_re = objects[k, 0]
        o_im = objects[k, 1]
        here = slice(k * side, (k + 1) * side)
        tall[:side, here] = probe_re * o_re - probe_im * o_im
        tall[side:, here] = probe_re * o_im + probe_im * o_re

    def turned(ref):
        top = jnp.concatenate([ref[:side, :side], ref[side:, :side]], axis=1)
        bottom = jnp.concatenate([ref[:side, side:], ref[side:, side:]], axis=1)
        return jnp.concatenate([top, bottom], axis=0)

    loads[1].wait()
    loads[2].wait()
    table = (high_ref[...], low_ref[...])
    flipped = (turned(high_ref), turned(low_ref))

    left = dot3(table, split(tall[...]))
    for k in range(count):
        here = slice(k * side, (k + 1) * side)
        wide[here, :side] = left[:side, here]
        wide[here, side:] = left[side:, here]
    spec = dot3(split(wide[...]), flipped)
    loads[3].wait()
    for k in range(count):
        here = slice(k * side, (k + 1) * side)
        s_re = spec[here, :side]
        s_im = spec[here, side:]
        norm = lax.rsqrt(jnp.maximum(s_re * s_re + s_im * s_im, 1.0))
        factor = 1.0 - amp_ref[k] * norm
        tall[:side, here] = s_re * factor
        tall[side:, here] = s_im * factor
    left = dot3(flipped, split(tall[...]))
    for k in range(count):
        here = slice(k * side, (k + 1) * side)
        wide[here, :side] = left[:side, here]
        wide[here, side:] = left[side:, here]
    back_ref[...] = dot3(split(wide[...]), table)

    sums = [jnp.zeros((side, side), F32)] * 3
    for k in range(count):
        here = slice(k * side, (k + 1) * side)
        o_re = objects[k, 0]
        o_im = objects[k, 1]
        b_re = back_ref[here, :side]
        b_im = back_ref[here, side:]
        sums[0] = sums[0] + (o_re * b_re + o_im * b_im)
        sums[1] = sums[1] + (o_re * b_im - o_im * b_re)
        sums[2] = sums[2] + (o_re * o_re + o_im * o_im)
    for j in range(3):
        term_ref[pl.ds(j, side, stride=3), :] = sums[j]


def deposit_kernel(
    row_ref, col_ref, cur_ref, probe_ref, back_ref, own_ref, up_ref, down_ref, grad
):
    side = probe_ref.shape[-1]
    half = side // 2
    rows = cur_ref.shape[1]
    lanes = cur_ref.shape[2]
    count = back_ref.shape[0] // side
    grad[...] = jnp.zeros(grad.shape, F32)
    probe_re = probe_ref[0]
    probe_im = probe_ref[1]
    for k in range(count):
        here = slice(k * side, (k + 1) * side)
        b_re = back_ref[here, :side]
        b_im = back_ref[here, side:]
        where, row_shift, col_shift = places(row_ref, col_ref, k, side, lanes)
        pair = (probe_re * b_re + probe_im * b_im, probe_re * b_im - probe_im * b_re)
        for c in range(2):
            block = jnp.concatenate([pair[c], jnp.zeros((8, side), F32)], axis=0)
            block = pltpu.roll(block, row_shift, 0)
            block = jnp.concatenate([block, jnp.zeros((side + 8, side), F32)], axis=1)
            block = pltpu.roll(block, col_shift, 1)
            grad[(c,) + where] = grad[(c,) + where] + block
    up_ref[...] = grad[:, :half]
    down_ref[...] = grad[:, half + rows :]
    own_ref[...] = cur_ref[...] - STEP_SIZE * grad[:, half : half + rows]


def update_kernel(own_ref, above_ref, below_ref, dh_ref, dl_ref, updated_ref, send_ref, whole, sheet):
    half = above_ref.shape[1]
    rows = own_ref.shape[1]
    per = dh_ref.shape[1]
    pieces = send_ref.shape[0] // (rows // 2)
    whole[:, half : rows - half] = own_ref[:, half : rows - half]
    whole[:, :half] = own_ref[:, :half] - STEP_SIZE * above_ref[...]
    whole[:, rows - half :] = own_ref[:, rows - half :] - STEP_SIZE * below_ref[...]
    updated_ref[...] = whole[...]
    table = (dh_ref[...], dl_ref[...])
    for c in range(2):
        product = dot3(split(whole[c]), table)
        for part in range(per // 128):
            sheet[part] = product[:, part * 128 : (part + 1) * 128]
        for s in range(2):
            for part in range(per // 128):
                piece = (2 * c + s) * (per // 128) + part
                rows_of = pl.ds(piece, rows // 2, stride=pieces)
                send_ref[rows_of, :] = sheet[part, pl.ds(s, rows // 2, stride=2), :]


def fold_kernel(share_ref, fold_ref):
    count = share_ref.shape[0] // 3
    fold_ref[...] = jnp.zeros(fold_ref.shape, F32)
    for j in range(3):
        total = jnp.sum(share_ref[pl.ds(j, count, stride=3), :], axis=0, keepdims=True)
        for t in range(fold_ref.shape[0] // 4):
            fold_ref[4 * t + j : 4 * t + j + 1, :] = total


def line_kernel(fold_ref, packed_ref, sent_ref):
    del packed_ref
    sums = [fold_ref[j : j + 1, :] for j in range(3)]
    for t in range(1, fold_ref.shape[0] // 4):
        for j in range(3):
            sums[j] = sums[j] + fold_ref[4 * t + j : 4 * t + j + 1, :]
    scale = lax.rsqrt(sums[2] + EPSILON)
    peers = fold_ref.shape[1]
    pieces = sent_ref.shape[0] // peers
    for j in range(2):
        line = jnp.broadcast_to(sums[j] * scale, (peers, peers))
        sent_ref[pl.ds(pieces - 2 + j, peers, stride=pieces), :] = line


def volume_kernel(arrived_ref, ah_ref, al_ref, volume_ref, direction_ref):
    parts = volume_ref.shape[-1] // 128
    angles = ah_ref.shape[1]
    pieces = arrived_ref.shape[0] // angles
    table = (ah_ref[...], al_ref[...])
    for c in range(2):
        direction_ref[c] = arrived_ref[pl.ds(pieces - 2 + c, angles, stride=pieces), :]
        for s in range(2):
            blocks = [
                arrived_ref[pl.ds((2 * c + s) * parts + part, angles, stride=pieces), :]
                for part in range(parts)
            ]
            volume_ref[c, s] = dot3(table, split(jnp.concatenate(blocks, axis=1)))


def band(offset, weight, length):
    column = lax.broadcasted_iota(jnp.int32, (length, offset.shape[1]), 0)
    matrix = jnp.zeros(column.shape, F32)
    for step in range(weight.shape[0]):
        matrix = jnp.where(column == offset + step, weight[step : step + 1], matrix)
    return matrix


def band_kernel(do_ref, dw_ref, ao_ref, aw_ref, dh_ref, dl_ref, ah_ref, al_ref):
    dh_ref[...], dl_ref[...] = split(band(do_ref[...], dw_ref[...], dh_ref.shape[0]))
    turned = band(ao_ref[...], aw_ref[...], ah_ref.shape[1])
    ah_ref[...], al_ref[...] = split(turned.T)


def held(value):
    return pltpu.with_memory_space_constraint(value, pltpu.VMEM)


def stay(value):
    return pltpu.with_memory_space_constraint(value, pltpu.HBM)


def vmem(count):
    return [pl.BlockSpec(memory_space=pltpu.VMEM)] * count


def local(
    projection, probe, amplitude, pos_row, pos_col, ang_offset, ang_weight, det_offset, det_weight
):
    side = probe.shape[-1]
    half = side // 2
    rows = projection.shape[2]
    lanes = projection.shape[3]
    count = amplitude.shape[1]
    angles = lax.axis_size("angle")
    tiles = lax.axis_size("tile")
    radial = det_offset.shape[0]
    up = [(i, i + 1) for i in range(tiles - 1)]
    down = [(i + 1, i) for i in range(tiles - 1)]

    current = projection[:, 0]
    shape = jax.ShapeDtypeStruct
    before = lax.ppermute(current[:, rows - half :], "tile", up)
    after = lax.ppermute(current[:, :half], "tile", down)

    regular = ang_offset.shape[0]
    det_high, det_low, ang_high, ang_low = pl.pallas_call(
        band_kernel,
        out_shape=(pltpu.VMEM((lanes, radial), BF16),) * 2
        + (pltpu.VMEM((regular, angles), BF16),) * 2,
        in_specs=vmem(4),
        out_specs=tuple(vmem(4)),
        name="bands",
        compiler_params=pltpu.CompilerParams(vmem_limit_bytes=8 << 20),
    )(det_offset[None], det_weight.T, ang_offset[None], ang_weight.T)

    high, low = complex_table(side)
    here = held(current)
    terms, back = pl.pallas_call(
        terms_kernel,
        out_shape=(pltpu.VMEM((3 * side, side), F32), pltpu.VMEM((count * side, 2 * side), F32)),
        in_specs=[pl.BlockSpec(memory_space=pltpu.SMEM)] * 2
        + vmem(3)
        + [pl.BlockSpec(memory_space=pltpu.HBM)] * 4,
        out_specs=tuple(vmem(2)),
        scratch_shapes=[
            pltpu.VMEM((2, rows + 2 * half, lanes), F32),
            pltpu.VMEM((count, 2, side, side), F32),
            pltpu.VMEM((2 * side, count * side), F32),
            pltpu.VMEM((count * side, 2 * side), F32),
            pltpu.VMEM((2, side, side), F32),
            pltpu.VMEM((count, side, side), F32),
            pltpu.VMEM((2 * side, 2 * side), BF16),
            pltpu.VMEM((2 * side, 2 * side), BF16),
            pltpu.SemaphoreType.DMA((4,)),
        ],
        name="terms",
        compiler_params=pltpu.CompilerParams(vmem_limit_bytes=20 << 20),
    )(
        pos_row, pos_col, here, held(before), held(after), stay(probe), stay(amplitude[0]),
        stay(jnp.asarray(high)), stay(jnp.asarray(low)),
    )

    shares = lax.all_to_all(terms.reshape(side, 3 * side), "angle", 0, 0, tiled=True)

    own, upper, lower = pl.pallas_call(
        deposit_kernel,
        out_shape=(
            pltpu.VMEM((2, rows, lanes), F32),
            pltpu.VMEM((2, half, lanes), F32),
            pltpu.VMEM((2, half, lanes), F32),
        ),
        in_specs=[pl.BlockSpec(memory_space=pltpu.SMEM)] * 2 + vmem(3),
        out_specs=tuple(vmem(3)),
        scratch_shapes=[pltpu.VMEM((2, rows + 2 * half, lanes), F32)],
        name="deposit",
        compiler_params=pltpu.CompilerParams(vmem_limit_bytes=12 << 20),
    )(pos_row, pos_col, here, held(probe), held(back))

    below = lax.ppermute(upper, "tile", down)
    above = lax.ppermute(lower, "tile", up)

    peers = rows // 2
    pieces = 4 * radial // 128 + 2
    updated, packed = pl.pallas_call(
        update_kernel,
        out_shape=(shape((2, rows, lanes), F32), pltpu.VMEM((peers * pieces, 128), F32)),
        in_specs=vmem(5),
        out_specs=tuple(vmem(2)),
        scratch_shapes=[
            pltpu.VMEM((2, rows, lanes), F32),
            pltpu.VMEM((radial // 128, rows, 128), F32),
        ],
        name="update",
        compiler_params=pltpu.CompilerParams(vmem_limit_bytes=12 << 20),
    )(held(own), held(above), held(below), held(det_high), held(det_low))

    folded = pl.pallas_call(
        fold_kernel,
        out_shape=pltpu.VMEM((4 * tiles, side), F32),
        in_specs=vmem(1),
        out_specs=vmem(1)[0],
        name="fold",
        compiler_params=pltpu.CompilerParams(vmem_limit_bytes=4 << 20),
    )(held(shares.reshape(3 * angles, side)))
    merged = lax.all_to_all(folded.reshape(tiles, 4 * side), "tile", 0, 0, tiled=True)
    sent = pl.pallas_call(
        line_kernel,
        out_shape=pltpu.VMEM((peers * pieces, 128), F32),
        in_specs=vmem(2),
        out_specs=vmem(1)[0],
        input_output_aliases={1: 0},
        name="line",
        compiler_params=pltpu.CompilerParams(vmem_limit_bytes=4 << 20),
    )(held(merged.reshape(4 * tiles, side)), held(packed))

    arrived = lax.all_to_all(
        sent.reshape(peers, pieces * 128), "angle", 0, 0, tiled=True
    )

    volume, direction = pl.pallas_call(
        volume_kernel,
        out_shape=(shape((2, 2, regular, radial), F32), shape((2, side, side), F32)),
        in_specs=vmem(3),
        out_specs=tuple(vmem(2)),
        name="volume",
        compiler_params=pltpu.CompilerParams(vmem_limit_bytes=8 << 20),
    )(held(arrived.reshape(angles * pieces, 128)), held(ang_high), held(ang_low))
    return (updated[:, None], direction, volume[:, None])


def solution(mesh):
    in_specs = (
        P(None, "angle", "tile", None),
        P(),
        P("angle", "tile", None, None),
        P("angle", "tile"),
        P("angle", "tile"),
        P(),
        P(),
        P(),
        P(),
    )
    out_specs = (P(None, "angle", "tile", None), P(), P(None, "tile", "angle", None, None))
    return jax.shard_map(local, mesh=mesh, in_specs=in_specs, out_specs=out_specs, check_vma=False)
```

```python
import functools

import jax
import jax.numpy as jnp
import numpy as np
from jax import lax
from jax.experimental import pallas as pl
from jax.experimental.pallas import tpu as pltpu
from jax.sharding import PartitionSpec as P

STEP_SIZE = 0.1
EPSILON = 1e-06
LINE = 16
F32 = jnp.float32
BF16 = jnp.bfloat16


def complex_table(length):
    counter = np.arange(length)
    angle = (counter[:, None] * counter[None, :] % length) * (2.0 * np.pi / length)
    re = np.cos(angle) / np.sqrt(length)
    im = -np.sin(angle) / np.sqrt(length)
    table = np.block([[re, -im], [im, re]]).astype(np.float32)
    high = table.astype(BF16)
    low = (table - high.astype(np.float32)).astype(BF16)
    return high, low


def split(value):
    high = value.astype(BF16)
    low = (value - high.astype(F32)).astype(BF16)
    return high, low


def dot3(left, right):
    mul = functools.partial(jnp.dot, preferred_element_type=F32)
    return mul(left[0], right[0]) + (mul(left[0], right[1]) + mul(left[1], right[0]))


def places(row_ref, col_ref, k, side, lanes):
    row = row_ref[0, k]
    col = col_ref[0, k]
    first = lax.div(row, 8)
    base = jnp.minimum(lax.div(col, side), lanes // side - 2)
    where = (
        pl.ds(pl.multiple_of(first * 8, 8), side + 8),
        pl.ds(pl.multiple_of(base * side, side), 2 * side),
    )
    return where, row - first * 8, col - base * side


def terms_kernel(
    row_ref, col_ref, cur_ref, before_ref, after_ref, probe_in, amp_in, high_in, low_in,
    term_ref, back_ref,
    padded, objects, tall, wide, probe_ref, amp_ref, high_ref, low_ref, sems,
):
    side = probe_ref.shape[-1]
    half = side // 2
    rows = cur_ref.shape[1]
    lanes = cur_ref.shape[2]
    count = amp_ref.shape[0]
    loads = [
        pltpu.make_async_copy(source, target, sems.at[i])
        for i, (source, target) in enumerate(
            ((probe_in, probe_ref), (high_in, high_ref), (low_in, low_ref), (amp_in, amp_ref))
        )
    ]
    for load in loads:
        load.start()

    padded[:, :half] = before_ref[...]
    padded[:, half : half + rows] = cur_ref[...]
    padded[:, half + rows :] = after_ref[...]

    loads[0].wait()
    probe_re = probe_ref[0]
    probe_im = probe_ref[1]
    for k in range(count):
        where, row_shift, col_shift = places(row_ref, col_ref, k, side, lanes)
        row_back = lax.rem(side + 8 - row_shift, side + 8)
        col_back = lax.rem(2 * side - col_shift, 2 * side)
        for c in range(2):
            block = padded[(c,) + where]
            block = pltpu.roll(block, col_back, 1)[:, :side]
            objects[k, c] = pltpu.roll(block, row_back, 0)[:side]
        o_re = objects[k, 0]
        o_im = objects[k, 1]
        here = slice(k * side, (k + 1) * side)
        tall[:side, here] = probe_re * o_re - probe_im * o_im
        tall[side:, here] = probe_re * o_im + probe_im * o_re

    def turned(ref):
        top = jnp.concatenate([ref[:side, :side], ref[side:, :side]], axis=1)
        bottom = jnp.concatenate([ref[:side, side:], ref[side:, side:]], axis=1)
        return jnp.concatenate([top, bottom], axis=0)

    loads[1].wait()
    loads[2].wait()
    table = (high_ref[...], low_ref[...])
    flipped = (turned(high_ref), turned(low_ref))

    left = dot3(table, split(tall[...]))
    for k in range(count):
        here = slice(k * side, (k + 1) * side)
        wide[here, :side] = left[:side, here]
        wide[here, side:] = left[side:, here]
    spec = dot3(split(wide[...]), flipped)
    loads[3].wait()
    for k in range(count):
        here = slice(k * side, (k + 1) * side)
        s_re = spec[here, :side]
        s_im = spec[here, side:]
        norm = lax.rsqrt(jnp.maximum(s_re * s_re + s_im * s_im, 1.0))
        factor = 1.0 - amp_ref[k] * norm
        tall[:side, here] = s_re * factor
        tall[side:, here] = s_im * factor
    left = dot3(flipped, split(tall[...]))
    for k in range(count):
        here = slice(k * side, (k + 1) * side)
        wide[here, :side] = left[:side, here]
        wide[here, side:] = left[side:, here]
    back_ref[...] = dot3(split(wide[...]), table)

    sums = [jnp.zeros((side, side), F32)] * 3
    for k in range(count):
        here = slice(k * side, (k + 1) * side)
        o_re = objects[k, 0]
        o_im = objects[k, 1]
        b_re = back_ref[here, :side]
        b_im = back_ref[here, side:]
        sums[0] = sums[0] + (o_re * b_re + o_im * b_im)
        sums[1] = sums[1] + (o_re * b_im - o_im * b_re)
        sums[2] = sums[2] + (o_re * o_re + o_im * o_im)
    for j in range(3):
        term_ref[pl.ds(j, side, stride=3), :] = sums[j]


def deposit_kernel(
    row_ref, col_ref, cur_ref, probe_ref, back_ref, own_ref, up_ref, down_ref, grad
):
    side = probe_ref.shape[-1]
    half = side // 2
    rows = cur_ref.shape[1]
    lanes = cur_ref.shape[2]
    count = back_ref.shape[0] // side
    grad[...] = jnp.zeros(grad.shape, F32)
    probe_re = probe_ref[0]
    probe_im = probe_ref[1]
    for k in range(count):
        here = slice(k * side, (k + 1) * side)
        b_re = back_ref[here, :side]
        b_im = back_ref[here, side:]
        where, row_shift, col_shift = places(row_ref, col_ref, k, side, lanes)
        pair = (probe_re * b_re + probe_im * b_im, probe_re * b_im - probe_im * b_re)
        for c in range(2):
            block = jnp.concatenate([pair[c], jnp.zeros((8, side), F32)], axis=0)
            block = pltpu.roll(block, row_shift, 0)
            block = jnp.concatenate([block, jnp.zeros((side + 8, side), F32)], axis=1)
            block = pltpu.roll(block, col_shift, 1)
            grad[(c,) + where] = grad[(c,) + where] + block
    up_ref[...] = grad[:, :half]
    down_ref[...] = grad[:, half + rows :]
    own_ref[...] = cur_ref[...] - STEP_SIZE * grad[:, half : half + rows]


def update_kernel(own_ref, above_ref, below_ref, dh_ref, dl_ref, updated_ref, send_ref, whole, sheet):
    half = above_ref.shape[1]
    rows = own_ref.shape[1]
    parts = dh_ref.shape[1] // 128
    chunk = send_ref.shape[0] // LINE
    whole[:, half : rows - half] = own_ref[:, half : rows - half]
    whole[:, :half] = own_ref[:, :half] - STEP_SIZE * above_ref[...]
    whole[:, rows - half :] = own_ref[:, rows - half :] - STEP_SIZE * below_ref[...]
    updated_ref[...] = whole[...]
    table = (dh_ref[...], dl_ref[...])
    for c in range(2):
        product = dot3(split(whole[c]), table)
        for part in range(parts):
            sheet[part] = product[:, part * 128 : (part + 1) * 128]
        for s in range(2):
            for part in range(parts):
                piece = (2 * c + s) * parts + part
                for g in range(rows // 2 // LINE):
                    source = pl.ds(2 * LINE * g + s, LINE, stride=2)
                    target = pl.ds(4 * parts * g + piece, LINE, stride=chunk)
                    send_ref[target, :] = sheet[part, source, :]


def gather_kernel(share_ref, sum_ref):
    count = share_ref.shape[0] // sum_ref.shape[0]
    step = sum_ref.shape[0]
    total = share_ref[:step, :]
    for i in range(1, count):
        total = total + share_ref[i * step : (i + 1) * step, :]
    sum_ref[...] = total


def fold_kernel(share_ref, fold_ref):
    count = share_ref.shape[0] // 3
    fold_ref[...] = jnp.zeros(fold_ref.shape, F32)
    for j in range(3):
        total = jnp.sum(share_ref[pl.ds(j, count, stride=3), :], axis=0, keepdims=True)
        for t in range(fold_ref.shape[0] // 4):
            fold_ref[4 * t + j : 4 * t + j + 1, :] = total


def line_kernel(fold_ref, packed_ref, sent_ref):
    del packed_ref
    sums = [fold_ref[j : j + 1, :] for j in range(3)]
    for t in range(1, fold_ref.shape[0] // 4):
        for j in range(3):
            sums[j] = sums[j] + fold_ref[4 * t + j : 4 * t + j + 1, :]
    scale = lax.rsqrt(sums[2] + EPSILON)
    chunk = sent_ref.shape[0] // LINE
    for j in range(2):
        line = jnp.broadcast_to(sums[j] * scale, (LINE, fold_ref.shape[1]))
        sent_ref[pl.ds(chunk - 2 + j, LINE, stride=chunk), :] = line


def turn_kernel(arrived_ref, sent_ref):
    old = arrived_ref.shape[0] // LINE
    pieces = 8
    groups = (old - 2) // pieces
    new = LINE * (pieces + 2)
    for g in range(groups):
        for j in range(pieces):
            block = arrived_ref[pl.ds(g * pieces + j, LINE, stride=old), :]
            sent_ref[pl.ds(g * new + j, LINE, stride=pieces), :] = block
    for c in range(2):
        block = arrived_ref[pl.ds(old - 2 + c, LINE, stride=old), :]
        for g in range(groups):
            sent_ref[pl.ds(g * new + LINE * pieces + c, LINE, stride=2), :] = block


def volume_kernel(arrived_ref, ah_ref, al_ref, volume_ref, direction_ref):
    parts = volume_ref.shape[-1] // 128
    pieces = 4 * parts
    groups = ah_ref.shape[1] // LINE
    new = arrived_ref.shape[0] // groups
    table = (ah_ref[...], al_ref[...])
    for c in range(2):
        for g in range(groups):
            source = pl.ds(g * new + LINE * pieces + c, LINE, stride=2)
            direction_ref[c, LINE * g : LINE * (g + 1), :] = arrived_ref[source, :]
        for s in range(2):
            columns = []
            for part in range(parts):
                piece = (2 * c + s) * parts + part
                blocks = [
                    arrived_ref[pl.ds(g * new + piece, LINE, stride=pieces), :]
                    for g in range(groups)
                ]
                columns.append(jnp.concatenate(blocks, axis=0))
            volume_ref[c, s] = dot3(table, split(jnp.concatenate(columns, axis=1)))


def band(offset, weight, length):
    column = lax.broadcasted_iota(jnp.int32, (length, offset.shape[1]), 0)
    matrix = jnp.zeros(column.shape, F32)
    for step in range(weight.shape[0]):
        matrix = jnp.where(column == offset + step, weight[step : step + 1], matrix)
    return matrix


def band_kernel(do_ref, dw_ref, ao_ref, aw_ref, dh_ref, dl_ref, ah_ref, al_ref):
    dh_ref[...], dl_ref[...] = split(band(do_ref[...], dw_ref[...], dh_ref.shape[0]))
    turned = band(ao_ref[...], aw_ref[...], ah_ref.shape[1])
    ah_ref[...], al_ref[...] = split(turned.T)


def held(value):
    return pltpu.with_memory_space_constraint(value, pltpu.VMEM)


def stay(value):
    return pltpu.with_memory_space_constraint(value, pltpu.HBM)


def vmem(count):
    return [pl.BlockSpec(memory_space=pltpu.VMEM)] * count


def local(
    projection, probe, amplitude, pos_row, pos_col, ang_offset, ang_weight, det_offset, det_weight
):
    side = probe.shape[-1]
    half = side // 2
    rows = projection.shape[2]
    lanes = projection.shape[3]
    count = amplitude.shape[1]
    angles = lax.axis_size("angle")
    tiles = lax.axis_size("tile")
    radial = det_offset.shape[0]
    up = [(i, i + 1) for i in range(tiles - 1)]
    down = [(i + 1, i) for i in range(tiles - 1)]

    groups = angles // LINE
    along = [[g * LINE + i for i in range(LINE)] for g in range(groups)]
    across = [[g * LINE + i for g in range(groups)] for i in range(LINE)]

    current = projection[:, 0]
    shape = jax.ShapeDtypeStruct
    before = lax.ppermute(current[:, rows - half :], "tile", up)
    after = lax.ppermute(current[:, :half], "tile", down)

    regular = ang_offset.shape[0]
    det_high, det_low, ang_high, ang_low = pl.pallas_call(
        band_kernel,
        out_shape=(pltpu.VMEM((lanes, radial), BF16),) * 2
        + (pltpu.VMEM((regular, angles), BF16),) * 2,
        in_specs=vmem(4),
        out_specs=tuple(vmem(4)),
        name="bands",
        compiler_params=pltpu.CompilerParams(vmem_limit_bytes=8 << 20),
    )(det_offset[None], det_weight.T, ang_offset[None], ang_weight.T)

    high, low = complex_table(side)
    here = held(current)
    terms, back = pl.pallas_call(
        terms_kernel,
        out_shape=(pltpu.VMEM((3 * side, side), F32), pltpu.VMEM((count * side, 2 * side), F32)),
        in_specs=[pl.BlockSpec(memory_space=pltpu.SMEM)] * 2
        + vmem(3)
        + [pl.BlockSpec(memory_space=pltpu.HBM)] * 4,
        out_specs=tuple(vmem(2)),
        scratch_shapes=[
            pltpu.VMEM((2, rows + 2 * half, lanes), F32),
            pltpu.VMEM((count, 2, side, side), F32),
            pltpu.VMEM((2 * side, count * side), F32),
            pltpu.VMEM((count * side, 2 * side), F32),
            pltpu.VMEM((2, side, side), F32),
            pltpu.VMEM((count, side, side), F32),
            pltpu.VMEM((2 * side, 2 * side), BF16),
            pltpu.VMEM((2 * side, 2 * side), BF16),
            pltpu.SemaphoreType.DMA((4,)),
        ],
        name="terms",
        compiler_params=pltpu.CompilerParams(vmem_limit_bytes=20 << 20),
    )(
        pos_row, pos_col, here, held(before), held(after), stay(probe), stay(amplitude[0]),
        stay(jnp.asarray(high)), stay(jnp.asarray(low)),
    )

    shares = lax.all_to_all(
        terms, "angle", 0, 0, tiled=True, axis_index_groups=across
    )

    own, upper, lower = pl.pallas_call(
        deposit_kernel,
        out_shape=(
            pltpu.VMEM((2, rows, lanes), F32),
            pltpu.VMEM((2, half, lanes), F32),
            pltpu.VMEM((2, half, lanes), F32),
        ),
        in_specs=[pl.BlockSpec(memory_space=pltpu.SMEM)] * 2 + vmem(3),
        out_specs=tuple(vmem(3)),
        scratch_shapes=[pltpu.VMEM((2, rows + 2 * half, lanes), F32)],
        name="deposit",
        compiler_params=pltpu.CompilerParams(vmem_limit_bytes=12 << 20),
    )(pos_row, pos_col, here, held(probe), held(back))

    below = lax.ppermute(upper, "tile", down)
    above = lax.ppermute(lower, "tile", up)

    gathered = pl.pallas_call(
        gather_kernel,
        out_shape=pltpu.VMEM((3 * LINE, side), F32),
        in_specs=vmem(1),
        out_specs=vmem(1)[0],
        name="gather",
        compiler_params=pltpu.CompilerParams(vmem_limit_bytes=4 << 20),
    )(held(shares))
    seconds = lax.all_to_all(
        gathered.reshape(LINE, 3 * side), "angle", 0, 0, tiled=True, axis_index_groups=along
    )

    pieces = 4 * radial // 128
    chunk = groups * pieces + 2
    updated, packed = pl.pallas_call(
        update_kernel,
        out_shape=(shape((2, rows, lanes), F32), pltpu.VMEM((LINE * chunk, 128), F32)),
        in_specs=vmem(5),
        out_specs=tuple(vmem(2)),
        scratch_shapes=[
            pltpu.VMEM((2, rows, lanes), F32),
            pltpu.VMEM((radial // 128, rows, 128), F32),
        ],
        name="update",
        compiler_params=pltpu.CompilerParams(vmem_limit_bytes=12 << 20),
    )(held(own), held(above), held(below), held(det_high), held(det_low))

    folded = pl.pallas_call(
        fold_kernel,
        out_shape=pltpu.VMEM((4 * tiles, side), F32),
        in_specs=vmem(1),
        out_specs=vmem(1)[0],
        name="fold",
        compiler_params=pltpu.CompilerParams(vmem_limit_bytes=4 << 20),
    )(held(seconds.reshape(3 * LINE, side)))
    merged = lax.all_to_all(folded.reshape(tiles, 4 * side), "tile", 0, 0, tiled=True)
    sent = pl.pallas_call(
        line_kernel,
        out_shape=pltpu.VMEM((LINE * chunk, 128), F32),
        in_specs=vmem(2),
        out_specs=vmem(1)[0],
        input_output_aliases={1: 0},
        name="line",
        compiler_params=pltpu.CompilerParams(vmem_limit_bytes=4 << 20),
    )(held(merged.reshape(4 * tiles, side)), held(packed))

    arrived = lax.all_to_all(
        sent.reshape(LINE, chunk * 128), "angle", 0, 0, tiled=True, axis_index_groups=along
    )
    block = LINE * (pieces + 2)
    turned = pl.pallas_call(
        turn_kernel,
        out_shape=pltpu.VMEM((groups * block, 128), F32),
        in_specs=vmem(1),
        out_specs=vmem(1)[0],
        name="turn",
        compiler_params=pltpu.CompilerParams(vmem_limit_bytes=4 << 20),
    )(held(arrived.reshape(LINE * chunk, 128)))
    landed = lax.all_to_all(turned, "angle", 0, 0, tiled=True, axis_index_groups=across)

    volume, direction = pl.pallas_call(
        volume_kernel,
        out_shape=(shape((2, 2, regular, radial), F32), shape((2, side, side), F32)),
        in_specs=vmem(3),
        out_specs=tuple(vmem(2)),
        name="volume",
        compiler_params=pltpu.CompilerParams(vmem_limit_bytes=8 << 20),
    )(held(landed), held(ang_high), held(ang_low))
    return (updated[:, None], direction, volume[:, None])


def solution(mesh):
    in_specs = (
        P(None, "angle", "tile", None),
        P(),
        P("angle", "tile", None, None),
        P("angle", "tile"),
        P("angle", "tile"),
        P(),
        P(),
        P(),
        P(),
    )
    out_specs = (P(None, "angle", "tile", None), P(), P(None, "tile", "angle", None, None))
    return jax.shard_map(local, mesh=mesh, in_specs=in_specs, out_specs=out_specs, check_vma=False)
```

```python
import functools

import jax
import jax.numpy as jnp
import numpy as np
from jax import lax
from jax.experimental import pallas as pl
from jax.experimental.pallas import tpu as pltpu
from jax.sharding import PartitionSpec as P

STEP_SIZE = 0.1
EPSILON = 1e-06
LINE = 16
F32 = jnp.float32
BF16 = jnp.bfloat16


def complex_table(length):
    counter = np.arange(length)
    angle = (counter[:, None] * counter[None, :] % length) * (2.0 * np.pi / length)
    re = np.cos(angle) / np.sqrt(length)
    im = -np.sin(angle) / np.sqrt(length)
    table = np.block([[re, -im], [im, re]]).astype(np.float32)
    high = table.astype(BF16)
    low = (table - high.astype(np.float32)).astype(BF16)
    return high, low


def split(value):
    high = value.astype(BF16)
    low = (value - high.astype(F32)).astype(BF16)
    return high, low


def dot3(left, right):
    mul = functools.partial(jnp.dot, preferred_element_type=F32)
    return mul(left[0], right[0]) + (mul(left[0], right[1]) + mul(left[1], right[0]))


def places(row_ref, col_ref, k, side, lanes):
    row = row_ref[0, k]
    col = col_ref[0, k]
    first = lax.div(row, 8)
    base = jnp.minimum(lax.div(col, side), lanes // side - 2)
    where = (
        pl.ds(pl.multiple_of(first * 8, 8), side + 8),
        pl.ds(pl.multiple_of(base * side, side), 2 * side),
    )
    return where, row - first * 8, col - base * side


def terms_kernel(
    row_ref, col_ref, cur_ref, before_ref, after_ref, probe_in, amp_in, high_in, low_in,
    term_ref, back_ref,
    padded, objects, tall, wide, probe_ref, amp_ref, high_ref, low_ref, sems,
):
    side = probe_ref.shape[-1]
    half = side // 2
    rows = cur_ref.shape[1]
    lanes = cur_ref.shape[2]
    count = amp_ref.shape[0]
    loads = [
        pltpu.make_async_copy(source, target, sems.at[i])
        for i, (source, target) in enumerate(
            ((probe_in, probe_ref), (high_in, high_ref), (low_in, low_ref), (amp_in, amp_ref))
        )
    ]
    for load in loads:
        load.start()

    padded[:, :half] = before_ref[...]
    padded[:, half : half + rows] = cur_ref[...]
    padded[:, half + rows :] = after_ref[...]

    loads[0].wait()
    probe_re = probe_ref[0]
    probe_im = probe_ref[1]
    for k in range(count):
        where, row_shift, col_shift = places(row_ref, col_ref, k, side, lanes)
        row_back = lax.rem(side + 8 - row_shift, side + 8)
        col_back = lax.rem(2 * side - col_shift, 2 * side)
        for c in range(2):
            block = padded[(c,) + where]
            block = pltpu.roll(block, col_back, 1)[:, :side]
            objects[k, c] = pltpu.roll(block, row_back, 0)[:side]
        o_re = objects[k, 0]
        o_im = objects[k, 1]
        here = slice(k * side, (k + 1) * side)
        tall[:side, here] = probe_re * o_re - probe_im * o_im
        tall[side:, here] = probe_re * o_im + probe_im * o_re

    def turned(ref):
        top = jnp.concatenate([ref[:side, :side], ref[side:, :side]], axis=1)
        bottom = jnp.concatenate([ref[:side, side:], ref[side:, side:]], axis=1)
        return jnp.concatenate([top, bottom], axis=0)

    loads[1].wait()
    loads[2].wait()
    table = (high_ref[...], low_ref[...])
    flipped = (turned(high_ref), turned(low_ref))

    left = dot3(table, split(tall[...]))
    for k in range(count):
        here = slice(k * side, (k + 1) * side)
        wide[here, :side] = left[:side, here]
        wide[here, side:] = left[side:, here]
    spec = dot3(split(wide[...]), flipped)
    loads[3].wait()
    for k in range(count):
        here = slice(k * side, (k + 1) * side)
        s_re = spec[here, :side]
        s_im = spec[here, side:]
        norm = lax.rsqrt(jnp.maximum(s_re * s_re + s_im * s_im, 1.0))
        factor = 1.0 - amp_ref[k] * norm
        tall[:side, here] = s_re * factor
        tall[side:, here] = s_im * factor
    left = dot3(flipped, split(tall[...]))
    for k in range(count):
        here = slice(k * side, (k + 1) * side)
        wide[here, :side] = left[:side, here]
        wide[here, side:] = left[side:, here]
    back_ref[...] = dot3(split(wide[...]), table)

    sums = [jnp.zeros((side, side), F32)] * 3
    for k in range(count):
        here = slice(k * side, (k + 1) * side)
        o_re = objects[k, 0]
        o_im = objects[k, 1]
        b_re = back_ref[here, :side]
        b_im = back_ref[here, side:]
        sums[0] = sums[0] + (o_re * b_re + o_im * b_im)
        sums[1] = sums[1] + (o_re * b_im - o_im * b_re)
        sums[2] = sums[2] + (o_re * o_re + o_im * o_im)
    for j in range(3):
        term_ref[pl.ds(j, side, stride=3), :] = sums[j]


def deposit_kernel(
    row_ref, col_ref, cur_ref, probe_ref, back_ref, own_ref, up_ref, down_ref, grad
):
    side = probe_ref.shape[-1]
    half = side // 2
    rows = cur_ref.shape[1]
    lanes = cur_ref.shape[2]
    count = back_ref.shape[0] // side
    grad[...] = jnp.zeros(grad.shape, F32)
    probe_re = probe_ref[0]
    probe_im = probe_ref[1]
    for k in range(count):
        here = slice(k * side, (k + 1) * side)
        b_re = back_ref[here, :side]
        b_im = back_ref[here, side:]
        where, row_shift, col_shift = places(row_ref, col_ref, k, side, lanes)
        pair = (probe_re * b_re + probe_im * b_im, probe_re * b_im - probe_im * b_re)
        for c in range(2):
            block = jnp.concatenate([pair[c], jnp.zeros((8, side), F32)], axis=0)
            block = pltpu.roll(block, row_shift, 0)
            block = jnp.concatenate([block, jnp.zeros((side + 8, side), F32)], axis=1)
            block = pltpu.roll(block, col_shift, 1)
            grad[(c,) + where] = grad[(c,) + where] + block
    up_ref[...] = grad[:, :half]
    down_ref[...] = grad[:, half + rows :]
    own_ref[...] = cur_ref[...] - STEP_SIZE * grad[:, half : half + rows]


def update_kernel(own_ref, above_ref, below_ref, dh_ref, dl_ref, updated_ref, send_ref, whole, sheet):
    half = above_ref.shape[1]
    rows = own_ref.shape[1]
    per = dh_ref.shape[1]
    pieces = send_ref.shape[0] // (rows // 2)
    whole[:, half : rows - half] = own_ref[:, half : rows - half]
    whole[:, :half] = own_ref[:, :half] - STEP_SIZE * above_ref[...]
    whole[:, rows - half :] = own_ref[:, rows - half :] - STEP_SIZE * below_ref[...]
    updated_ref[...] = whole[...]
    table = (dh_ref[...], dl_ref[...])
    for c in range(2):
        product = dot3(split(whole[c]), table)
        for part in range(per // 128):
            sheet[part] = product[:, part * 128 : (part + 1) * 128]
        for s in range(2):
            for part in range(per // 128):
                piece = (2 * c + s) * (per // 128) + part
                rows_of = pl.ds(piece, rows // 2, stride=pieces)
                send_ref[rows_of, :] = sheet[part, pl.ds(s, rows // 2, stride=2), :]


def gather_kernel(share_ref, sum_ref):
    count = share_ref.shape[0] // sum_ref.shape[0]
    step = sum_ref.shape[0]
    total = share_ref[:step, :]
    for i in range(1, count):
        total = total + share_ref[i * step : (i + 1) * step, :]
    sum_ref[...] = total


def fold_kernel(share_ref, fold_ref):
    count = share_ref.shape[0] // 3
    fold_ref[...] = jnp.zeros(fold_ref.shape, F32)
    for j in range(3):
        total = jnp.sum(share_ref[pl.ds(j, count, stride=3), :], axis=0, keepdims=True)
        for t in range(fold_ref.shape[0] // 4):
            fold_ref[4 * t + j : 4 * t + j + 1, :] = total


def line_kernel(fold_ref, packed_ref, sent_ref):
    del packed_ref
    sums = [fold_ref[j : j + 1, :] for j in range(3)]
    for t in range(1, fold_ref.shape[0] // 4):
        for j in range(3):
            sums[j] = sums[j] + fold_ref[4 * t + j : 4 * t + j + 1, :]
    scale = lax.rsqrt(sums[2] + EPSILON)
    peers = fold_ref.shape[1]
    pieces = sent_ref.shape[0] // peers
    for j in range(2):
        line = jnp.broadcast_to(sums[j] * scale, (peers, peers))
        sent_ref[pl.ds(pieces - 2 + j, peers, stride=pieces), :] = line


def volume_kernel(arrived_ref, ah_ref, al_ref, volume_ref, direction_ref):
    parts = volume_ref.shape[-1] // 128
    angles = ah_ref.shape[1]
    pieces = arrived_ref.shape[0] // angles
    table = (ah_ref[...], al_ref[...])
    for c in range(2):
        direction_ref[c] = arrived_ref[pl.ds(pieces - 2 + c, angles, stride=pieces), :]
        for s in range(2):
            blocks = [
                arrived_ref[pl.ds((2 * c + s) * parts + part, angles, stride=pieces), :]
                for part in range(parts)
            ]
            volume_ref[c, s] = dot3(table, split(jnp.concatenate(blocks, axis=1)))


def band(offset, weight, length):
    column = lax.broadcasted_iota(jnp.int32, (length, offset.shape[1]), 0)
    matrix = jnp.zeros(column.shape, F32)
    for step in range(weight.shape[0]):
        matrix = jnp.where(column == offset + step, weight[step : step + 1], matrix)
    return matrix


def band_kernel(do_ref, dw_ref, ao_ref, aw_ref, dh_ref, dl_ref, ah_ref, al_ref):
    dh_ref[...], dl_ref[...] = split(band(do_ref[...], dw_ref[...], dh_ref.shape[0]))
    turned = band(ao_ref[...], aw_ref[...], ah_ref.shape[1])
    ah_ref[...], al_ref[...] = split(turned.T)


def held(value):
    return pltpu.with_memory_space_constraint(value, pltpu.VMEM)


def stay(value):
    return pltpu.with_memory_space_constraint(value, pltpu.HBM)


def vmem(count):
    return [pl.BlockSpec(memory_space=pltpu.VMEM)] * count


def local(
    projection, probe, amplitude, pos_row, pos_col, ang_offset, ang_weight, det_offset, det_weight
):
    side = probe.shape[-1]
    half = side // 2
    rows = projection.shape[2]
    lanes = projection.shape[3]
    count = amplitude.shape[1]
    angles = lax.axis_size("angle")
    tiles = lax.axis_size("tile")
    radial = det_offset.shape[0]
    up = [(i, i + 1) for i in range(tiles - 1)]
    down = [(i + 1, i) for i in range(tiles - 1)]

    groups = angles // LINE
    across = [[g * LINE + i for g in range(groups)] for i in range(LINE)]
    along = [[g * LINE + i for i in range(LINE)] for g in range(groups)]

    current = projection[:, 0]
    shape = jax.ShapeDtypeStruct
    before = lax.ppermute(current[:, rows - half :], "tile", up)
    after = lax.ppermute(current[:, :half], "tile", down)

    regular = ang_offset.shape[0]
    det_high, det_low, ang_high, ang_low = pl.pallas_call(
        band_kernel,
        out_shape=(pltpu.VMEM((lanes, radial), BF16),) * 2
        + (pltpu.VMEM((regular, angles), BF16),) * 2,
        in_specs=vmem(4),
        out_specs=tuple(vmem(4)),
        name="bands",
        compiler_params=pltpu.CompilerParams(vmem_limit_bytes=8 << 20),
    )(det_offset[None], det_weight.T, ang_offset[None], ang_weight.T)

    high, low = complex_table(side)
    here = held(current)
    terms, back = pl.pallas_call(
        terms_kernel,
        out_shape=(pltpu.VMEM((3 * side, side), F32), pltpu.VMEM((count * side, 2 * side), F32)),
        in_specs=[pl.BlockSpec(memory_space=pltpu.SMEM)] * 2
        + vmem(3)
        + [pl.BlockSpec(memory_space=pltpu.HBM)] * 4,
        out_specs=tuple(vmem(2)),
        scratch_shapes=[
            pltpu.VMEM((2, rows + 2 * half, lanes), F32),
            pltpu.VMEM((count, 2, side, side), F32),
            pltpu.VMEM((2 * side, count * side), F32),
            pltpu.VMEM((count * side, 2 * side), F32),
            pltpu.VMEM((2, side, side), F32),
            pltpu.VMEM((count, side, side), F32),
            pltpu.VMEM((2 * side, 2 * side), BF16),
            pltpu.VMEM((2 * side, 2 * side), BF16),
            pltpu.SemaphoreType.DMA((4,)),
        ],
        name="terms",
        compiler_params=pltpu.CompilerParams(vmem_limit_bytes=20 << 20),
    )(
        pos_row, pos_col, here, held(before), held(after), stay(probe), stay(amplitude[0]),
        stay(jnp.asarray(high)), stay(jnp.asarray(low)),
    )

    shares = lax.all_to_all(
        terms, "angle", 0, 0, tiled=True, axis_index_groups=across
    )

    own, upper, lower = pl.pallas_call(
        deposit_kernel,
        out_shape=(
            pltpu.VMEM((2, rows, lanes), F32),
            pltpu.VMEM((2, half, lanes), F32),
            pltpu.VMEM((2, half, lanes), F32),
        ),
        in_specs=[pl.BlockSpec(memory_space=pltpu.SMEM)] * 2 + vmem(3),
        out_specs=tuple(vmem(3)),
        scratch_shapes=[pltpu.VMEM((2, rows + 2 * half, lanes), F32)],
        name="deposit",
        compiler_params=pltpu.CompilerParams(vmem_limit_bytes=12 << 20),
    )(pos_row, pos_col, here, held(probe), held(back))

    below = lax.ppermute(upper, "tile", down)
    above = lax.ppermute(lower, "tile", up)

    gathered = pl.pallas_call(
        gather_kernel,
        out_shape=pltpu.VMEM((3 * LINE, side), F32),
        in_specs=vmem(1),
        out_specs=vmem(1)[0],
        name="gather",
        compiler_params=pltpu.CompilerParams(vmem_limit_bytes=4 << 20),
    )(held(shares))
    seconds = lax.all_to_all(
        gathered.reshape(LINE, 3 * side), "angle", 0, 0, tiled=True, axis_index_groups=along
    )

    peers = rows // 2
    pieces = 4 * radial // 128 + 2
    updated, packed = pl.pallas_call(
        update_kernel,
        out_shape=(shape((2, rows, lanes), F32), pltpu.VMEM((peers * pieces, 128), F32)),
        in_specs=vmem(5),
        out_specs=tuple(vmem(2)),
        scratch_shapes=[
            pltpu.VMEM((2, rows, lanes), F32),
            pltpu.VMEM((radial // 128, rows, 128), F32),
        ],
        name="update",
        compiler_params=pltpu.CompilerParams(vmem_limit_bytes=12 << 20),
    )(held(own), held(above), held(below), held(det_high), held(det_low))

    folded = pl.pallas_call(
        fold_kernel,
        out_shape=pltpu.VMEM((4 * tiles, side), F32),
        in_specs=vmem(1),
        out_specs=vmem(1)[0],
        name="fold",
        compiler_params=pltpu.CompilerParams(vmem_limit_bytes=4 << 20),
    )(held(seconds.reshape(3 * LINE, side)))
    merged = lax.all_to_all(folded.reshape(tiles, 4 * side), "tile", 0, 0, tiled=True)
    sent = pl.pallas_call(
        line_kernel,
        out_shape=pltpu.VMEM((peers * pieces, 128), F32),
        in_specs=vmem(2),
        out_specs=vmem(1)[0],
        input_output_aliases={1: 0},
        name="line",
        compiler_params=pltpu.CompilerParams(vmem_limit_bytes=4 << 20),
    )(held(merged.reshape(4 * tiles, side)), held(packed))

    arrived = lax.all_to_all(
        sent.reshape(peers, pieces * 128), "angle", 0, 0, tiled=True
    )

    volume, direction = pl.pallas_call(
        volume_kernel,
        out_shape=(shape((2, 2, regular, radial), F32), shape((2, side, side), F32)),
        in_specs=vmem(3),
        out_specs=tuple(vmem(2)),
        name="volume",
        compiler_params=pltpu.CompilerParams(vmem_limit_bytes=8 << 20),
    )(held(arrived.reshape(angles * pieces, 128)), held(ang_high), held(ang_low))
    return (updated[:, None], direction, volume[:, None])


def solution(mesh):
    in_specs = (
        P(None, "angle", "tile", None),
        P(),
        P("angle", "tile", None, None),
        P("angle", "tile"),
        P("angle", "tile"),
        P(),
        P(),
        P(),
        P(),
    )
    out_specs = (P(None, "angle", "tile", None), P(), P(None, "tile", "angle", None, None))
    return jax.shard_map(local, mesh=mesh, in_specs=in_specs, out_specs=out_specs, check_vma=False)
```

```python
import functools

import jax
import jax.numpy as jnp
import numpy as np
from jax import lax
from jax.experimental import pallas as pl
from jax.experimental.pallas import tpu as pltpu
from jax.sharding import PartitionSpec as P

STEP_SIZE = 0.1
EPSILON = 1e-06
LINE = 16
F32 = jnp.float32
BF16 = jnp.bfloat16


def complex_table(length):
    counter = np.arange(length)
    angle = (counter[:, None] * counter[None, :] % length) * (2.0 * np.pi / length)
    re = np.cos(angle) / np.sqrt(length)
    im = -np.sin(angle) / np.sqrt(length)
    table = np.block([[re, -im], [im, re]]).astype(np.float32)
    high = table.astype(BF16)
    low = (table - high.astype(np.float32)).astype(BF16)
    return high, low


def split(value):
    high = value.astype(BF16)
    low = (value - high.astype(F32)).astype(BF16)
    return high, low


def dot3(left, right):
    mul = functools.partial(jnp.dot, preferred_element_type=F32)
    return mul(left[0], right[0]) + (mul(left[0], right[1]) + mul(left[1], right[0]))


def places(row_ref, col_ref, k, side, lanes):
    row = row_ref[0, k]
    col = col_ref[0, k]
    first = lax.div(row, 8)
    base = jnp.minimum(lax.div(col, side), lanes // side - 2)
    where = (
        pl.ds(pl.multiple_of(first * 8, 8), side + 8),
        pl.ds(pl.multiple_of(base * side, side), 2 * side),
    )
    return where, row - first * 8, col - base * side


def terms_kernel(
    row_ref, col_ref, cur_ref, before_ref, after_ref, probe_in, amp_in, high_in, low_in,
    term_ref, back_ref,
    padded, objects, tall, wide, probe_ref, amp_ref, high_ref, low_ref, sems,
):
    side = probe_ref.shape[-1]
    half = side // 2
    rows = cur_ref.shape[1]
    lanes = cur_ref.shape[2]
    count = amp_ref.shape[0]
    loads = [
        pltpu.make_async_copy(source, target, sems.at[i])
        for i, (source, target) in enumerate(
            ((probe_in, probe_ref), (high_in, high_ref), (low_in, low_ref), (amp_in, amp_ref))
        )
    ]
    for load in loads:
        load.start()

    padded[:, :half] = before_ref[...]
    padded[:, half : half + rows] = cur_ref[...]
    padded[:, half + rows :] = after_ref[...]

    loads[0].wait()
    probe_re = probe_ref[0]
    probe_im = probe_ref[1]
    for k in range(count):
        where, row_shift, col_shift = places(row_ref, col_ref, k, side, lanes)
        row_back = lax.rem(side + 8 - row_shift, side + 8)
        col_back = lax.rem(2 * side - col_shift, 2 * side)
        for c in range(2):
            block = padded[(c,) + where]
            block = pltpu.roll(block, col_back, 1)[:, :side]
            objects[k, c] = pltpu.roll(block, row_back, 0)[:side]
        o_re = objects[k, 0]
        o_im = objects[k, 1]
        here = slice(k * side, (k + 1) * side)
        tall[:side, here] = probe_re * o_re - probe_im * o_im
        tall[side:, here] = probe_re * o_im + probe_im * o_re

    def turned(ref):
        top = jnp.concatenate([ref[:side, :side], ref[side:, :side]], axis=1)
        bottom = jnp.concatenate([ref[:side, side:], ref[side:, side:]], axis=1)
        return jnp.concatenate([top, bottom], axis=0)

    loads[1].wait()
    loads[2].wait()
    table = (high_ref[...], low_ref[...])
    flipped = (turned(high_ref), turned(low_ref))

    left = dot3(table, split(tall[...]))
    for k in range(count):
        here = slice(k * side, (k + 1) * side)
        wide[here, :side] = left[:side, here]
        wide[here, side:] = left[side:, here]
    spec = dot3(split(wide[...]), flipped)
    loads[3].wait()
    for k in range(count):
        here = slice(k * side, (k + 1) * side)
        s_re = spec[here, :side]
        s_im = spec[here, side:]
        norm = lax.rsqrt(jnp.maximum(s_re * s_re + s_im * s_im, 1.0))
        factor = 1.0 - amp_ref[k] * norm
        tall[:side, here] = s_re * factor
        tall[side:, here] = s_im * factor
    left = dot3(flipped, split(tall[...]))
    for k in range(count):
        here = slice(k * side, (k + 1) * side)
        wide[here, :side] = left[:side, here]
        wide[here, side:] = left[side:, here]
    back_ref[...] = dot3(split(wide[...]), table)

    sums = [jnp.zeros((side, side), F32)] * 3
    for k in range(count):
        here = slice(k * side, (k + 1) * side)
        o_re = objects[k, 0]
        o_im = objects[k, 1]
        b_re = back_ref[here, :side]
        b_im = back_ref[here, side:]
        sums[0] = sums[0] + (o_re * b_re + o_im * b_im)
        sums[1] = sums[1] + (o_re * b_im - o_im * b_re)
        sums[2] = sums[2] + (o_re * o_re + o_im * o_im)
    for j in range(3):
        term_ref[pl.ds(j, side, stride=3), :] = sums[j]


def deposit_kernel(
    row_ref, col_ref, cur_ref, probe_ref, back_ref, own_ref, up_ref, down_ref, grad
):
    side = probe_ref.shape[-1]
    half = side // 2
    rows = cur_ref.shape[1]
    lanes = cur_ref.shape[2]
    count = back_ref.shape[0] // side
    grad[...] = jnp.zeros(grad.shape, F32)
    probe_re = probe_ref[0]
    probe_im = probe_ref[1]
    for k in range(count):
        here = slice(k * side, (k + 1) * side)
        b_re = back_ref[here, :side]
        b_im = back_ref[here, side:]
        where, row_shift, col_shift = places(row_ref, col_ref, k, side, lanes)
        pair = (probe_re * b_re + probe_im * b_im, probe_re * b_im - probe_im * b_re)
        for c in range(2):
            block = jnp.concatenate([pair[c], jnp.zeros((8, side), F32)], axis=0)
            block = pltpu.roll(block, row_shift, 0)
            block = jnp.concatenate([block, jnp.zeros((side + 8, side), F32)], axis=1)
            block = pltpu.roll(block, col_shift, 1)
            grad[(c,) + where] = grad[(c,) + where] + block
    up_ref[...] = grad[:, :half]
    down_ref[...] = grad[:, half + rows :]
    own_ref[...] = cur_ref[...] - STEP_SIZE * grad[:, half : half + rows]


def update_kernel(own_ref, above_ref, below_ref, dh_ref, dl_ref, updated_ref, send_ref, whole, sheet):
    half = above_ref.shape[1]
    rows = own_ref.shape[1]
    per = dh_ref.shape[1]
    pieces = send_ref.shape[0] // (rows // 2)
    whole[:, half : rows - half] = own_ref[:, half : rows - half]
    whole[:, :half] = own_ref[:, :half] - STEP_SIZE * above_ref[...]
    whole[:, rows - half :] = own_ref[:, rows - half :] - STEP_SIZE * below_ref[...]
    updated_ref[...] = whole[...]
    table = (dh_ref[...], dl_ref[...])
    for c in range(2):
        product = dot3(split(whole[c]), table)
        for part in range(per // 128):
            sheet[part] = product[:, part * 128 : (part + 1) * 128]
        for s in range(2):
            for part in range(per // 128):
                piece = (2 * c + s) * (per // 128) + part
                rows_of = pl.ds(piece, rows // 2, stride=pieces)
                send_ref[rows_of, :] = sheet[part, pl.ds(s, rows // 2, stride=2), :]


def gather_kernel(share_ref, sum_ref):
    tiles = sum_ref.shape[0] // (3 * LINE)
    step = 3 * LINE
    count = share_ref.shape[0] // step
    for j in range(3):
        total = share_ref[pl.ds(j, LINE, stride=3), :]
        for i in range(1, count):
            total = total + share_ref[pl.ds(i * step + j, LINE, stride=3), :]
        for t in range(tiles):
            sum_ref[pl.ds(3 * t + j, LINE, stride=3 * tiles), :] = total


def line_kernel(share_ref, packed_ref, sent_ref):
    del packed_ref
    count = share_ref.shape[0] // 3
    sums = [
        jnp.sum(share_ref[pl.ds(j, count, stride=3), :], axis=0, keepdims=True) for j in range(3)
    ]
    scale = lax.rsqrt(sums[2] + EPSILON)
    peers = share_ref.shape[1]
    pieces = sent_ref.shape[0] // peers
    for j in range(2):
        line = jnp.broadcast_to(sums[j] * scale, (peers, peers))
        sent_ref[pl.ds(pieces - 2 + j, peers, stride=pieces), :] = line


def volume_kernel(arrived_ref, ah_ref, al_ref, volume_ref, direction_ref):
    parts = volume_ref.shape[-1] // 128
    angles = ah_ref.shape[1]
    pieces = arrived_ref.shape[0] // angles
    table = (ah_ref[...], al_ref[...])
    for c in range(2):
        direction_ref[c] = arrived_ref[pl.ds(pieces - 2 + c, angles, stride=pieces), :]
        for s in range(2):
            blocks = [
                arrived_ref[pl.ds((2 * c + s) * parts + part, angles, stride=pieces), :]
                for part in range(parts)
            ]
            volume_ref[c, s] = dot3(table, split(jnp.concatenate(blocks, axis=1)))


def band(offset, weight, length):
    column = lax.broadcasted_iota(jnp.int32, (length, offset.shape[1]), 0)
    matrix = jnp.zeros(column.shape, F32)
    for step in range(weight.shape[0]):
        matrix = jnp.where(column == offset + step, weight[step : step + 1], matrix)
    return matrix


def band_kernel(do_ref, dw_ref, ao_ref, aw_ref, dh_ref, dl_ref, ah_ref, al_ref):
    dh_ref[...], dl_ref[...] = split(band(do_ref[...], dw_ref[...], dh_ref.shape[0]))
    turned = band(ao_ref[...], aw_ref[...], ah_ref.shape[1])
    ah_ref[...], al_ref[...] = split(turned.T)


def held(value):
    return pltpu.with_memory_space_constraint(value, pltpu.VMEM)


def stay(value):
    return pltpu.with_memory_space_constraint(value, pltpu.HBM)


def vmem(count):
    return [pl.BlockSpec(memory_space=pltpu.VMEM)] * count


def local(
    projection, probe, amplitude, pos_row, pos_col, ang_offset, ang_weight, det_offset, det_weight
):
    side = probe.shape[-1]
    half = side // 2
    rows = projection.shape[2]
    lanes = projection.shape[3]
    count = amplitude.shape[1]
    angles = lax.axis_size("angle")
    tiles = lax.axis_size("tile")
    radial = det_offset.shape[0]
    up = [(i, i + 1) for i in range(tiles - 1)]
    down = [(i + 1, i) for i in range(tiles - 1)]

    groups = angles // LINE
    across = [[g * LINE + i for g in range(groups)] for i in range(LINE)]
    block = LINE * tiles
    along = [[g * block + i for i in range(block)] for g in range(groups)]

    current = projection[:, 0]
    shape = jax.ShapeDtypeStruct
    before = lax.ppermute(current[:, rows - half :], "tile", up)
    after = lax.ppermute(current[:, :half], "tile", down)

    regular = ang_offset.shape[0]
    det_high, det_low, ang_high, ang_low = pl.pallas_call(
        band_kernel,
        out_shape=(pltpu.VMEM((lanes, radial), BF16),) * 2
        + (pltpu.VMEM((regular, angles), BF16),) * 2,
        in_specs=vmem(4),
        out_specs=tuple(vmem(4)),
        name="bands",
        compiler_params=pltpu.CompilerParams(vmem_limit_bytes=8 << 20),
    )(det_offset[None], det_weight.T, ang_offset[None], ang_weight.T)

    high, low = complex_table(side)
    here = held(current)
    terms, back = pl.pallas_call(
        terms_kernel,
        out_shape=(pltpu.VMEM((3 * side, side), F32), pltpu.VMEM((count * side, 2 * side), F32)),
        in_specs=[pl.BlockSpec(memory_space=pltpu.SMEM)] * 2
        + vmem(3)
        + [pl.BlockSpec(memory_space=pltpu.HBM)] * 4,
        out_specs=tuple(vmem(2)),
        scratch_shapes=[
            pltpu.VMEM((2, rows + 2 * half, lanes), F32),
            pltpu.VMEM((count, 2, side, side), F32),
            pltpu.VMEM((2 * side, count * side), F32),
            pltpu.VMEM((count * side, 2 * side), F32),
            pltpu.VMEM((2, side, side), F32),
            pltpu.VMEM((count, side, side), F32),
            pltpu.VMEM((2 * side, 2 * side), BF16),
            pltpu.VMEM((2 * side, 2 * side), BF16),
            pltpu.SemaphoreType.DMA((4,)),
        ],
        name="terms",
        compiler_params=pltpu.CompilerParams(vmem_limit_bytes=20 << 20),
    )(
        pos_row, pos_col, here, held(before), held(after), stay(probe), stay(amplitude[0]),
        stay(jnp.asarray(high)), stay(jnp.asarray(low)),
    )

    shares = lax.all_to_all(
        terms, "angle", 0, 0, tiled=True, axis_index_groups=across
    )

    own, upper, lower = pl.pallas_call(
        deposit_kernel,
        out_shape=(
            pltpu.VMEM((2, rows, lanes), F32),
            pltpu.VMEM((2, half, lanes), F32),
            pltpu.VMEM((2, half, lanes), F32),
        ),
        in_specs=[pl.BlockSpec(memory_space=pltpu.SMEM)] * 2 + vmem(3),
        out_specs=tuple(vmem(3)),
        scratch_shapes=[pltpu.VMEM((2, rows + 2 * half, lanes), F32)],
        name="deposit",
        compiler_params=pltpu.CompilerParams(vmem_limit_bytes=12 << 20),
    )(pos_row, pos_col, here, held(probe), held(back))

    below = lax.ppermute(upper, "tile", down)
    above = lax.ppermute(lower, "tile", up)

    gathered = pl.pallas_call(
        gather_kernel,
        out_shape=pltpu.VMEM((3 * block, side), F32),
        in_specs=vmem(1),
        out_specs=vmem(1)[0],
        name="gather",
        compiler_params=pltpu.CompilerParams(vmem_limit_bytes=4 << 20),
    )(held(shares))
    seconds = lax.all_to_all(
        gathered.reshape(block, 3 * side), ("angle", "tile"), 0, 0,
        tiled=True, axis_index_groups=along,
    )

    peers = rows // 2
    pieces = 4 * radial // 128 + 2
    updated, packed = pl.pallas_call(
        update_kernel,
        out_shape=(shape((2, rows, lanes), F32), pltpu.VMEM((peers * pieces, 128), F32)),
        in_specs=vmem(5),
        out_specs=tuple(vmem(2)),
        scratch_shapes=[
            pltpu.VMEM((2, rows, lanes), F32),
            pltpu.VMEM((radial // 128, rows, 128), F32),
        ],
        name="update",
        compiler_params=pltpu.CompilerParams(vmem_limit_bytes=12 << 20),
    )(held(own), held(above), held(below), held(det_high), held(det_low))

    sent = pl.pallas_call(
        line_kernel,
        out_shape=pltpu.VMEM((peers * pieces, 128), F32),
        in_specs=vmem(2),
        out_specs=vmem(1)[0],
        input_output_aliases={1: 0},
        name="line",
        compiler_params=pltpu.CompilerParams(vmem_limit_bytes=4 << 20),
    )(held(seconds.reshape(3 * block, side)), held(packed))

    arrived = lax.all_to_all(
        sent.reshape(peers, pieces * 128), "angle", 0, 0, tiled=True
    )

    volume, direction = pl.pallas_call(
        volume_kernel,
        out_shape=(shape((2, 2, regular, radial), F32), shape((2, side, side), F32)),
        in_specs=vmem(3),
        out_specs=tuple(vmem(2)),
        name="volume",
        compiler_params=pltpu.CompilerParams(vmem_limit_bytes=8 << 20),
    )(held(arrived.reshape(angles * pieces, 128)), held(ang_high), held(ang_low))
    return (updated[:, None], direction, volume[:, None])


def solution(mesh):
    in_specs = (
        P(None, "angle", "tile", None),
        P(),
        P("angle", "tile", None, None),
        P("angle", "tile"),
        P("angle", "tile"),
        P(),
        P(),
        P(),
        P(),
    )
    out_specs = (P(None, "angle", "tile", None), P(), P(None, "tile", "angle", None, None))
    return jax.shard_map(local, mesh=mesh, in_specs=in_specs, out_specs=out_specs, check_vma=False)
```

```python
import functools

import jax
import jax.numpy as jnp
import numpy as np
from jax import lax
from jax.experimental import pallas as pl
from jax.experimental.pallas import tpu as pltpu
from jax.sharding import PartitionSpec as P

STEP_SIZE = 0.1
EPSILON = 1e-06
LINE = 16
CORES = 2
F32 = jnp.float32
BF16 = jnp.bfloat16


def complex_table(length):
    counter = np.arange(length)
    angle = (counter[:, None] * counter[None, :] % length) * (2.0 * np.pi / length)
    re = np.cos(angle) / np.sqrt(length)
    im = -np.sin(angle) / np.sqrt(length)
    table = np.block([[re, -im], [im, re]]).astype(np.float32)
    high = table.astype(BF16)
    low = (table - high.astype(np.float32)).astype(BF16)
    return high, low


def split(value):
    high = value.astype(BF16)
    low = (value - high.astype(F32)).astype(BF16)
    return high, low


def dot3(left, right):
    mul = functools.partial(jnp.dot, preferred_element_type=F32)
    return mul(left[0], right[0]) + (mul(left[0], right[1]) + mul(left[1], right[0]))


def places(row_ref, col_ref, k, side, lanes):
    row = row_ref[0, k]
    col = col_ref[0, k]
    first = lax.div(row, 8)
    base = jnp.minimum(lax.div(col, side), lanes // side - 2)
    where = (
        pl.ds(pl.multiple_of(first * 8, 8), side + 8),
        pl.ds(pl.multiple_of(base * side, side), 2 * side),
    )
    return where, row - first * 8, col - base * side


def terms_kernel(
    row_ref, col_ref, cur_ref, before_ref, after_ref, probe_in, amp_in, high_in, low_in,
    term_ref, back_ref,
    padded, objects, tall, wide, probe_ref, amp_ref, high_ref, low_ref, sems,
):
    side = probe_ref.shape[-1]
    half = side // 2
    rows = cur_ref.shape[1]
    lanes = cur_ref.shape[2]
    count = amp_ref.shape[0]
    loads = [
        pltpu.make_async_copy(source, target, sems.at[i])
        for i, (source, target) in enumerate(
            ((probe_in, probe_ref), (high_in, high_ref), (low_in, low_ref), (amp_in, amp_ref))
        )
    ]
    for load in loads:
        load.start()

    padded[:, :half] = before_ref[...]
    padded[:, half : half + rows] = cur_ref[...]
    padded[:, half + rows :] = after_ref[...]

    loads[0].wait()
    probe_re = probe_ref[0]
    probe_im = probe_ref[1]
    for k in range(count):
        where, row_shift, col_shift = places(row_ref, col_ref, k, side, lanes)
        row_back = lax.rem(side + 8 - row_shift, side + 8)
        col_back = lax.rem(2 * side - col_shift, 2 * side)
        for c in range(2):
            block = padded[(c,) + where]
            block = pltpu.roll(block, col_back, 1)[:, :side]
            objects[k, c] = pltpu.roll(block, row_back, 0)[:side]
        o_re = objects[k, 0]
        o_im = objects[k, 1]
        here = slice(k * side, (k + 1) * side)
        tall[:side, here] = probe_re * o_re - probe_im * o_im
        tall[side:, here] = probe_re * o_im + probe_im * o_re

    def turned(ref):
        top = jnp.concatenate([ref[:side, :side], ref[side:, :side]], axis=1)
        bottom = jnp.concatenate([ref[:side, side:], ref[side:, side:]], axis=1)
        return jnp.concatenate([top, bottom], axis=0)

    loads[1].wait()
    loads[2].wait()
    table = (high_ref[...], low_ref[...])
    flipped = (turned(high_ref), turned(low_ref))

    left = dot3(table, split(tall[...]))
    for k in range(count):
        here = slice(k * side, (k + 1) * side)
        wide[here, :side] = left[:side, here]
        wide[here, side:] = left[side:, here]
    spec = dot3(split(wide[...]), flipped)
    loads[3].wait()
    for k in range(count):
        here = slice(k * side, (k + 1) * side)
        s_re = spec[here, :side]
        s_im = spec[here, side:]
        norm = lax.rsqrt(jnp.maximum(s_re * s_re + s_im * s_im, 1.0))
        factor = 1.0 - amp_ref[k] * norm
        tall[:side, here] = s_re * factor
        tall[side:, here] = s_im * factor
    left = dot3(flipped, split(tall[...]))
    for k in range(count):
        here = slice(k * side, (k + 1) * side)
        wide[here, :side] = left[:side, here]
        wide[here, side:] = left[side:, here]
    back_ref[...] = dot3(split(wide[...]), table)

    sums = [jnp.zeros((side, side), F32)] * 3
    for k in range(count):
        here = slice(k * side, (k + 1) * side)
        o_re = objects[k, 0]
        o_im = objects[k, 1]
        b_re = back_ref[here, :side]
        b_im = back_ref[here, side:]
        sums[0] = sums[0] + (o_re * b_re + o_im * b_im)
        sums[1] = sums[1] + (o_re * b_im - o_im * b_re)
        sums[2] = sums[2] + (o_re * o_re + o_im * o_im)
    step = 3 * LINE
    for j in range(3):
        for i in range(term_ref.shape[0] // step):
            first = i // CORES * LINE
            term_ref[pl.ds(i * step + j, LINE, stride=3), :] = sums[j][first : first + LINE]


def deposit_kernel(
    row_ref, col_ref, cur_ref, probe_ref, back_ref, own_ref, up_ref, down_ref, grad
):
    side = probe_ref.shape[-1]
    half = side // 2
    rows = cur_ref.shape[1]
    lanes = cur_ref.shape[2]
    count = back_ref.shape[0] // side
    grad[...] = jnp.zeros(grad.shape, F32)
    probe_re = probe_ref[0]
    probe_im = probe_ref[1]
    for k in range(count):
        here = slice(k * side, (k + 1) * side)
        b_re = back_ref[here, :side]
        b_im = back_ref[here, side:]
        where, row_shift, col_shift = places(row_ref, col_ref, k, side, lanes)
        pair = (probe_re * b_re + probe_im * b_im, probe_re * b_im - probe_im * b_re)
        for c in range(2):
            block = jnp.concatenate([pair[c], jnp.zeros((8, side), F32)], axis=0)
            block = pltpu.roll(block, row_shift, 0)
            block = jnp.concatenate([block, jnp.zeros((side + 8, side), F32)], axis=1)
            block = pltpu.roll(block, col_shift, 1)
            grad[(c,) + where] = grad[(c,) + where] + block
    up_ref[...] = grad[:, :half]
    down_ref[...] = grad[:, half + rows :]
    own_ref[...] = cur_ref[...] - STEP_SIZE * grad[:, half : half + rows]


def update_kernel(own_ref, above_ref, below_ref, dh_ref, dl_ref, updated_ref, send_ref, whole, sheet):
    half = above_ref.shape[1]
    rows = own_ref.shape[1]
    per = dh_ref.shape[1]
    pieces = send_ref.shape[0] // (rows // 2)
    whole[:, half : rows - half] = own_ref[:, half : rows - half]
    whole[:, :half] = own_ref[:, :half] - STEP_SIZE * above_ref[...]
    whole[:, rows - half :] = own_ref[:, rows - half :] - STEP_SIZE * below_ref[...]
    updated_ref[...] = whole[...]
    table = (dh_ref[...], dl_ref[...])
    for c in range(2):
        product = dot3(split(whole[c]), table)
        for part in range(per // 128):
            sheet[part] = product[:, part * 128 : (part + 1) * 128]
        for s in range(2):
            for part in range(per // 128):
                piece = (2 * c + s) * (per // 128) + part
                rows_of = pl.ds(piece, rows // 2, stride=pieces)
                send_ref[rows_of, :] = sheet[part, pl.ds(s, rows // 2, stride=2), :]


def gather_kernel(share_ref, sum_ref):
    tiles = sum_ref.shape[0] // (3 * LINE)
    step = 3 * LINE
    count = share_ref.shape[0] // step
    for j in range(3):
        total = share_ref[pl.ds(j, LINE, stride=3), :]
        for i in range(1, count):
            total = total + share_ref[pl.ds(i * step + j, LINE, stride=3), :]
        for t in range(tiles):
            sum_ref[pl.ds(3 * t + j, LINE, stride=3 * tiles), :] = total


def line_kernel(share_ref, packed_ref, sent_ref):
    del packed_ref
    count = share_ref.shape[0] // 3
    sums = [
        jnp.sum(share_ref[pl.ds(j, count, stride=3), :], axis=0, keepdims=True) for j in range(3)
    ]
    scale = lax.rsqrt(sums[2] + EPSILON)
    peers = share_ref.shape[1]
    pieces = sent_ref.shape[0] // peers
    for j in range(2):
        line = jnp.broadcast_to(sums[j] * scale, (peers, peers))
        sent_ref[pl.ds(pieces - 2 + j, peers, stride=pieces), :] = line


def volume_kernel(arrived_ref, ah_ref, al_ref, volume_ref, direction_ref):
    parts = volume_ref.shape[-1] // 128
    angles = ah_ref.shape[1]
    pieces = arrived_ref.shape[0] // angles
    table = (ah_ref[...], al_ref[...])
    for c in range(2):
        direction_ref[c] = arrived_ref[pl.ds(pieces - 2 + c, angles, stride=pieces), :]
        for s in range(2):
            blocks = [
                arrived_ref[pl.ds((2 * c + s) * parts + part, angles, stride=pieces), :]
                for part in range(parts)
            ]
            volume_ref[c, s] = dot3(table, split(jnp.concatenate(blocks, axis=1)))


def band(offset, weight, length):
    column = lax.broadcasted_iota(jnp.int32, (length, offset.shape[1]), 0)
    matrix = jnp.zeros(column.shape, F32)
    for step in range(weight.shape[0]):
        matrix = jnp.where(column == offset + step, weight[step : step + 1], matrix)
    return matrix


def band_kernel(do_ref, dw_ref, ao_ref, aw_ref, dh_ref, dl_ref, ah_ref, al_ref):
    dh_ref[...], dl_ref[...] = split(band(do_ref[...], dw_ref[...], dh_ref.shape[0]))
    turned = band(ao_ref[...], aw_ref[...], ah_ref.shape[1])
    ah_ref[...], al_ref[...] = split(turned.T)


def held(value):
    return pltpu.with_memory_space_constraint(value, pltpu.VMEM)


def stay(value):
    return pltpu.with_memory_space_constraint(value, pltpu.HBM)


def vmem(count):
    return [pl.BlockSpec(memory_space=pltpu.VMEM)] * count


def local(
    projection, probe, amplitude, pos_row, pos_col, ang_offset, ang_weight, det_offset, det_weight
):
    side = probe.shape[-1]
    half = side // 2
    rows = projection.shape[2]
    lanes = projection.shape[3]
    count = amplitude.shape[1]
    angles = lax.axis_size("angle")
    tiles = lax.axis_size("tile")
    radial = det_offset.shape[0]
    up = [(i, i + 1) for i in range(tiles - 1)]
    down = [(i + 1, i) for i in range(tiles - 1)]

    groups = angles // LINE
    chips = tiles // CORES
    block = LINE * chips

    def member(g, z, chip, core):
        return (g * LINE + z) * tiles + chip * CORES + core

    across = [
        [member(g, z, chip, core) for g in range(groups) for core in range(CORES)]
        for z in range(LINE)
        for chip in range(chips)
    ]
    along = [
        [member(g, z, chip, core) for z in range(LINE) for chip in range(chips)]
        for g in range(groups)
        for core in range(CORES)
    ]

    current = projection[:, 0]
    shape = jax.ShapeDtypeStruct
    before = lax.ppermute(current[:, rows - half :], "tile", up)
    after = lax.ppermute(current[:, :half], "tile", down)

    regular = ang_offset.shape[0]
    det_high, det_low, ang_high, ang_low = pl.pallas_call(
        band_kernel,
        out_shape=(pltpu.VMEM((lanes, radial), BF16),) * 2
        + (pltpu.VMEM((regular, angles), BF16),) * 2,
        in_specs=vmem(4),
        out_specs=tuple(vmem(4)),
        name="bands",
        compiler_params=pltpu.CompilerParams(vmem_limit_bytes=8 << 20),
    )(det_offset[None], det_weight.T, ang_offset[None], ang_weight.T)

    high, low = complex_table(side)
    here = held(current)
    terms, back = pl.pallas_call(
        terms_kernel,
        out_shape=(
            pltpu.VMEM((3 * CORES * side, side), F32),
            pltpu.VMEM((count * side, 2 * side), F32),
        ),
        in_specs=[pl.BlockSpec(memory_space=pltpu.SMEM)] * 2
        + vmem(3)
        + [pl.BlockSpec(memory_space=pltpu.HBM)] * 4,
        out_specs=tuple(vmem(2)),
        scratch_shapes=[
            pltpu.VMEM((2, rows + 2 * half, lanes), F32),
            pltpu.VMEM((count, 2, side, side), F32),
            pltpu.VMEM((2 * side, count * side), F32),
            pltpu.VMEM((count * side, 2 * side), F32),
            pltpu.VMEM((2, side, side), F32),
            pltpu.VMEM((count, side, side), F32),
            pltpu.VMEM((2 * side, 2 * side), BF16),
            pltpu.VMEM((2 * side, 2 * side), BF16),
            pltpu.SemaphoreType.DMA((4,)),
        ],
        name="terms",
        compiler_params=pltpu.CompilerParams(vmem_limit_bytes=20 << 20),
    )(
        pos_row, pos_col, here, held(before), held(after), stay(probe), stay(amplitude[0]),
        stay(jnp.asarray(high)), stay(jnp.asarray(low)),
    )

    shares = lax.all_to_all(terms, ("angle", "tile"), 0, 0, tiled=True, axis_index_groups=across)

    own, upper, lower = pl.pallas_call(
        deposit_kernel,
        out_shape=(
            pltpu.VMEM((2, rows, lanes), F32),
            pltpu.VMEM((2, half, lanes), F32),
            pltpu.VMEM((2, half, lanes), F32),
        ),
        in_specs=[pl.BlockSpec(memory_space=pltpu.SMEM)] * 2 + vmem(3),
        out_specs=tuple(vmem(3)),
        scratch_shapes=[pltpu.VMEM((2, rows + 2 * half, lanes), F32)],
        name="deposit",
        compiler_params=pltpu.CompilerParams(vmem_limit_bytes=12 << 20),
    )(pos_row, pos_col, here, held(probe), held(back))

    below = lax.ppermute(upper, "tile", down)
    above = lax.ppermute(lower, "tile", up)

    gathered = pl.pallas_call(
        gather_kernel,
        out_shape=pltpu.VMEM((3 * block, side), F32),
        in_specs=vmem(1),
        out_specs=vmem(1)[0],
        name="gather",
        compiler_params=pltpu.CompilerParams(vmem_limit_bytes=4 << 20),
    )(held(shares))
    seconds = lax.all_to_all(
        gathered.reshape(block, 3 * side), ("angle", "tile"), 0, 0,
        tiled=True, axis_index_groups=along,
    )

    peers = rows // 2
    pieces = 4 * radial // 128 + 2
    updated, packed = pl.pallas_call(
        update_kernel,
        out_shape=(shape((2, rows, lanes), F32), pltpu.VMEM((peers * pieces, 128), F32)),
        in_specs=vmem(5),
        out_specs=tuple(vmem(2)),
        scratch_shapes=[
            pltpu.VMEM((2, rows, lanes), F32),
            pltpu.VMEM((radial // 128, rows, 128), F32),
        ],
        name="update",
        compiler_params=pltpu.CompilerParams(vmem_limit_bytes=12 << 20),
    )(held(own), held(above), held(below), held(det_high), held(det_low))

    sent = pl.pallas_call(
        line_kernel,
        out_shape=pltpu.VMEM((peers * pieces, 128), F32),
        in_specs=vmem(2),
        out_specs=vmem(1)[0],
        input_output_aliases={1: 0},
        name="line",
        compiler_params=pltpu.CompilerParams(vmem_limit_bytes=4 << 20),
    )(held(seconds.reshape(3 * block, side)), held(packed))

    arrived = lax.all_to_all(
        sent.reshape(peers, pieces * 128), "angle", 0, 0, tiled=True
    )

    volume, direction = pl.pallas_call(
        volume_kernel,
        out_shape=(shape((2, 2, regular, radial), F32), shape((2, side, side), F32)),
        in_specs=vmem(3),
        out_specs=tuple(vmem(2)),
        name="volume",
        compiler_params=pltpu.CompilerParams(vmem_limit_bytes=8 << 20),
    )(held(arrived.reshape(angles * pieces, 128)), held(ang_high), held(ang_low))
    return (updated[:, None], direction, volume[:, None])


def solution(mesh):
    in_specs = (
        P(None, "angle", "tile", None),
        P(),
        P("angle", "tile", None, None),
        P("angle", "tile"),
        P("angle", "tile"),
        P(),
        P(),
        P(),
        P(),
    )
    out_specs = (P(None, "angle", "tile", None), P(), P(None, "tile", "angle", None, None))
    return jax.shard_map(local, mesh=mesh, in_specs=in_specs, out_specs=out_specs, check_vma=False)
```
